512 devices in a mesh: wide: 64 (over y_hi, x, z), narrow: 8 (over y_lo, core).
Axes of the slice: x: 4, y: 8 (y_hi: 2, y_lo: 4; y = y_hi * 4 + y_lo), z: 8, core: 2. Of those that a mesh axis runs over, the one named last changes fastest.
Arguments:
- raw_ints: float32 [512, 512, 768], P('wide', 'narrow'), may hold values from -1.2 to 1.2
- metric: float32 [768, 768], P('narrow'), may hold values from -0.21875 to 0.21875
- occ_energy: float32 [512], P(('wide', 'narrow')), may hold values from -1.5 to -0.3
- vir_energy: float32 [512], replicated, may hold values from 0.3 to 3
- pair_kept: int32 [512], P(('wide', 'narrow')), may hold values 0 or 1
Outputs:
- density: float32 [512, 512], P('narrow')
- energy: float32 [512], P(('wide', 'narrow'))
The draws below stay inside these ranges and needn't reach their ends.
All inputs are finite; a program needn't handle non-finite values. No bound on the sum of `pair_kept` on one device may be relied on, other than what follows from the above.
Results may differ from the reference program's by a relative error of at most 0.0003.
Values sent between devices are 32-bit elements; how exact they have to be, the bound alone decides.
A program may use at most 64 MiB of HBM per device.

```python
import jax
import jax.numpy as jnp
from jax import lax

NAUX = 768
VIR = 512
OCC = 512
N_NARROW = 8


def set_ends(array, rng, least, largest):
    longest = array.shape.index(max(array.shape))
    spots = []
    for shift in (0, 1):
        where = [jax.random.randint(jax.random.fold_in(rng, axis), (), 0, length) for axis, length in enumerate(array.shape)]
        where[longest] = (where[longest] + shift) % array.shape[longest]
        spots.append(tuple(where))
    return array.at[spots[0]].set(least).at[spots[1]].set(largest)


def levels(rng, shape, shards, smallest, top_value):
    def one(position, shards_of):
        draws = jax.random.uniform(jax.random.fold_in(jax.random.fold_in(rng, 6), position), (shards_of,), jnp.float32, smallest / len(shards), top_value / len(shards))
        return jnp.repeat(jnp.exp(draws), shape[position] // shards_of).reshape((-1,) + (1,) * (len(shape) - position - 1))

    level = one(*shards[0])
    for cut in shards[1:]:
        level = level * one(*cut)
    return level


def centred(key, dims, spread, reach, pieces=(), held_as=jnp.bfloat16):
    factor_of = levels(key, dims, pieces, -0.22, 0.18) if pieces else 1.0
    drawn = jax.random.normal(key, dims, jnp.float32) * spread * factor_of
    return jnp.minimum(jnp.maximum(drawn, -reach), reach).astype(held_as)


def setup_inputs(seed: int = 0) -> dict:
    splits = jax.random.split(jax.random.key(seed), 6)
    raw_ints = centred(splits[0], (OCC, VIR, NAUX), 0.2, 1.2, ((0, 64), (1, 8)), jnp.float32)
    metric = centred(splits[1], (NAUX, NAUX), NAUX ** -0.5, 0.21875, ((0, 8),), jnp.float32)
    occ_energy = jnp.clip(-1.5 + 1.2 * jax.random.uniform(splits[2], (OCC,), jnp.float32) ** levels(splits[2], (OCC,), ((0, 512),), -0.2, 0.2), -1.5, -0.3)
    vir_energy = jnp.clip(jax.random.uniform(splits[3], (VIR,), jnp.float32, 0.3, 3.0), 0.3, 3.0)
    pair_kept = set_ends((jax.random.randint(splits[4], (OCC,), 0, 4) < 3).astype(jnp.int32), jax.random.fold_in(splits[4], 1), 0, 1)
    return {"raw_ints": raw_ints, "metric": metric, "occ_energy": occ_energy, "vir_energy": vir_energy, "pair_kept": pair_kept}


HIGHEST_PRECISION = lax.Precision.HIGHEST


def pair_pass(left_block, right_block, vir_energy, left_energy, right_energy):
    pair_ints = lax.dot_general(left_block, right_block, (((1,), (1,)), ((), ())), precision=HIGHEST_PRECISION, preferred_element_type=jnp.float32)
    denominator = (vir_energy[:, None] + vir_energy[None, :]) - left_energy - right_energy
    amplitude = pair_ints / denominator
    pair_value = -jnp.sum(pair_ints * (2.0 * amplitude - amplitude.T)) / (pair_ints.shape[0] * pair_ints.shape[1])
    return amplitude, pair_value


def reference(raw_ints, metric, occ_energy, vir_energy, pair_kept):
    fitted = jnp.einsum("iap,qp->iaq", raw_ints, metric, precision=HIGHEST_PRECISION)
    kept_mask = pair_kept.astype(jnp.float32)
    orbitals = fitted.shape[0]

    def accumulate(density, orbital):
        partner = ((orbital - N_NARROW) % orbitals).astype(jnp.int32)
        amplitude, pair_value = pair_pass(fitted[orbital], fitted[partner], vir_energy, occ_energy[orbital], occ_energy[partner])
        pair_term = lax.dot_general(amplitude, amplitude, (((1,), (1,)), ((), ())), precision=HIGHEST_PRECISION, preferred_element_type=jnp.float32)
        pair_term = pair_term + lax.dot_general(amplitude, amplitude, (((0,), (0,)), ((), ())), precision=HIGHEST_PRECISION, preferred_element_type=jnp.float32)
        return density + kept_mask[orbital] * pair_term, kept_mask[orbital] * pair_value

    density, pair_values = lax.scan(accumulate, jnp.zeros((VIR, VIR), jnp.float32), jnp.arange(orbitals, dtype=jnp.int32))
    energy = pair_values + jnp.roll(pair_values, -N_NARROW)
    return density * (0.0625 / orbitals), energy
```

```python
import functools

import jax
import jax.numpy as jnp
from jax import lax
from jax.experimental import pallas as pl
from jax.experimental.pallas import tpu as pltpu
from jax.sharding import PartitionSpec as P

MESH = pl.DeviceIdType.MESH
F32 = jnp.float32
BF16 = jnp.bfloat16

NX, NZ, NY, NARROW = 4, 8, 4, 8
PLANE = NX * NZ


def split(value):
    high = value.astype(BF16)
    return high, (value - high.astype(F32)).astype(BF16)


def dot_nt(left, right):
    return lax.dot_general(left, right, (((1,), (1,)), ((), ())), preferred_element_type=F32)


def dot3(left_hi, left_lo, right_hi, right_lo):
    return dot_nt(left_hi, right_hi) + (dot_nt(left_hi, right_lo) + dot_nt(left_lo, right_hi))


def kernel(
    n_wide, dens_scale,
    raw, metric, side, vir,
    dens_out, energy_out,
    rbuf, jbuf, mbuf, m_hi, m_lo, x_hi, x_lo, fi_hi, fi_lo, fj_hi, fj_lo,
    rinv, pbuf, abuf, c_hi, c_lo, dbuf, dpart, s0, xbuf, s1, zbuf, s2, ybuf, tbuf, ofull,
    side_in, pv_own, pv_in,
    loc_sem, a_s, a_r, f_s, f_r, m1_s, m1_r, m2_s, m2_r, m3_s, m3_r, side_sem, pv_sem,
    c_s, c_r, xs_s, xs_r, zs_s, zs_r, ys_s, ys_r, gz_s, gz_r, gx_s, gx_r,
):
    w = lax.axis_index("wide")
    n = lax.axis_index("narrow")
    y, c = n // 2, n % 2
    hi, plane = w // PLANE, w % PLANE
    x, z = plane // NZ, plane % NZ
    gy = hi * NY + y
    up = (w + 1) % n_wide
    down = (w + n_wide - 1) % n_wide
    fwd = (w + 1 - 2 * c + n_wide) % n_wide
    back = (w - 1 + 2 * c + n_wide) % n_wide

    def remote(src, dst, ss, rs, wide, narrow):
        return pltpu.make_async_remote_copy(
            src_ref=src, dst_ref=dst, send_sem=ss, recv_sem=rs,
            device_id=(wide, narrow), device_id_type=MESH,
        )

    def at_x(d):
        return hi * PLANE + ((x + d) % NX) * NZ + z

    def at_z(d):
        return hi * PLANE + x * NZ + (z + d) % NZ

    def at_y(d):
        there = (gy + d) % (2 * NY)
        return (there // NY) * PLANE + plane, 2 * (there % NY) + c

    peers = [(w, (n + d) % NARROW) for d in range(1, NARROW)]
    peers += [at_y(d) for d in range(1, 2 * NY)]
    peers += [(at_x(d), n) for d in range(1, NX)]
    peers += [(at_z(d), n) for d in range(1, NZ)]
    peers += [(up, n), (down, n)]
    barrier = pltpu.get_barrier_semaphore()
    for peer in peers:
        pl.semaphore_signal(barrier, inc=1, device_id=peer, device_id_type=MESH)
    pl.semaphore_wait(barrier, len(peers))

    rows_q = metric.shape[0] // NX
    own_rows = pl.ds(x * (NY * rows_q) + y * rows_q, rows_q)
    m1 = []
    for d in range(1, NY):
        copy = remote(
            metric.at[pl.ds(x * rows_q, rows_q)], mbuf.at[own_rows],
            m1_s.at[d], m1_r.at[d], w, 2 * ((y + d) % NY) + c,
        )
        copy.start()
        m1.append(copy)
    m_local = pltpu.make_async_copy(metric.at[pl.ds(x * rows_q, rows_q)], mbuf.at[own_rows], loc_sem.at[0])
    m_local.start()
    side_copy = remote(side, side_in, side_sem.at[0], side_sem.at[1], fwd, n)
    side_copy.start()

    a2a = [None]
    for d in range(1, NARROW):
        to = (n + d) % NARROW
        copy = remote(raw.at[to], rbuf.at[n], a_s.at[d], a_r.at[d], w, to)
        copy.start()
        a2a.append(copy)
    own_slot = pltpu.make_async_copy(raw.at[n], rbuf.at[n], loc_sem.at[1])
    own_slot.start()
    slots = [(n + NARROW - d) % NARROW for d in range(NARROW)]
    forwards = []

    def forward(d):
        src = raw.at[n] if d == 0 else rbuf.at[slots[d]]
        copy = remote(src, jbuf.at[slots[d]], f_s.at[d], f_r.at[d], fwd, n)
        copy.start()
        forwards.append(copy)

    forward(0)
    a2a[1].wait_recv()
    forward(1)

    m_local.wait()
    for copy in m1:
        copy.wait_recv()
    block = NY * rows_q
    half = NX * block
    m2 = []
    for d in range(1, NX):
        rows = pl.ds(x * block, block)
        copy = remote(mbuf.at[rows], mbuf.at[rows], m2_s.at[d], m2_r.at[d], at_x(d), n)
        copy.start()
        m2.append(copy)
    m3 = []

    def to_partner(d):
        which = (x + NX - d) % NX
        copy = remote(
            mbuf.at[pl.ds(which * block, block)], mbuf.at[pl.ds(half + which * block, block)],
            m3_s.at[d], m3_r.at[d], w, 2 * y + 1 - c,
        )
        copy.start()
        m3.append(copy)

    to_partner(0)

    side_copy.wait()
    virtuals = vir.shape[1]
    rinv[...] = jnp.broadcast_to(vir[...], (virtuals, virtuals))
    energies = side[0][:1, :1] + side_in[0][:1, :1]
    for r in range(0, virtuals, 128):
        across = rinv[:, r:r + 128].T
        pbuf[r:r + 128, :] = 1.0 / ((rinv[r:r + 128, :] + across) - energies)

    a2a[2].wait_recv()
    forward(2)
    a2a[3].wait_recv()
    forward(3)
    for d in range(1, NX):
        m2[d - 1].wait_recv()
        to_partner(d)
    a2a[4].wait_recv()
    forward(4)
    for copy in m3:
        copy.wait_recv()

    def split_rows(k, carry):
        rows = pl.ds(pl.multiple_of(k * 96, 96), 96)
        m_hi[rows, :], m_lo[rows, :] = split(mbuf[rows, :])
        return carry

    lax.fori_loop(0, mbuf.shape[0] // 96, split_rows, 0)

    def fit(src, f_hi, f_lo, four):
        for k, slot in enumerate(four):
            part = pl.ds(k * 64, 64)
            x_hi[part, :], x_lo[part, :] = split(src[slot])

        def tile(t, carry):
            cols = pl.ds(pl.multiple_of(t * 256, 256), 256)
            fitted = dot3(x_hi[...], x_lo[...], m_hi[cols, :], m_lo[cols, :])
            high, low = split(fitted)
            for k, slot in enumerate(four):
                f_hi[slot, :, cols] = high[k * 64:(k + 1) * 64]
                f_lo[slot, :, cols] = low[k * 64:(k + 1) * 64]
            return carry

        lax.fori_loop(0, mbuf.shape[0] // 256, tile, 0)

    own_slot.wait()
    fit(rbuf, fi_hi, fi_lo, slots[:4])
    a2a[5].wait_recv()
    forward(5)
    for d in range(4):
        forwards[d].wait_recv()
    fit(jbuf, fj_hi, fj_lo, slots[:4])
    a2a[6].wait_recv()
    forward(6)
    a2a[7].wait_recv()
    forward(7)
    fit(rbuf, fi_hi, fi_lo, slots[4:])
    for d in range(4, 8):
        forwards[d].wait_recv()
    fit(jbuf, fj_hi, fj_lo, slots[4:])

    rinv[...] = pbuf[...]

    def pair_tile(t, carry):
        ra, cb = t // 2, t % 2
        four_a, four_b = pl.ds(ra * 4, 4), pl.ds(cb * 4, 4)
        shape = (256, fi_hi.shape[2])
        ints = dot3(
            fi_hi[four_a].reshape(shape), fi_lo[four_a].reshape(shape),
            fj_hi[four_b].reshape(shape), fj_lo[four_b].reshape(shape),
        )
        rows = pl.ds(pl.multiple_of(ra * 256, 256), 256)
        cols = pl.ds(pl.multiple_of(cb * 256, 256), 256)
        pbuf[rows, cols] = ints
        abuf[rows, cols] = ints * rinv[rows, cols]
        return carry

    lax.fori_loop(0, 4, pair_tile, 0)

    def value_tile(t, total):
        ra, cb = t // 2, t % 2
        rows = pl.ds(pl.multiple_of(ra * 256, 256), 256)
        cols = pl.ds(pl.multiple_of(cb * 256, 256), 256)
        cols_t = pl.ds(pl.multiple_of(virtuals + cb * 256, 256), 256)
        amp = abuf[rows, cols]
        amp_t = abuf[cols, rows].T
        c_hi[rows, cols], c_lo[rows, cols] = split(amp)
        c_hi[rows, cols_t], c_lo[rows, cols_t] = split(amp_t)
        return total + jnp.sum(pbuf[rows, cols] * (2.0 * amp - amp_t), axis=0, keepdims=True)

    total = lax.fori_loop(0, 4, value_tile, jnp.zeros((1, 256), F32))
    kept = jnp.where(c == 0, side[1], side_in[1])
    pair_sum = jnp.sum(total, axis=1, keepdims=True)
    pv_own[...] = -kept * (jnp.broadcast_to(pair_sum, kept.shape) / (virtuals * virtuals))
    pv_copy = remote(pv_own, pv_in, pv_sem.at[0], pv_sem.at[1], back, n)
    pv_copy.start()

    scale = kept[:1, :1] * dens_scale

    def dens_tile(t, carry):
        ra, cb = t // 2, t % 2
        rows = pl.ds(pl.multiple_of(ra * 256, 256), 256)
        cols = pl.ds(pl.multiple_of(cb * 256, 256), 256)
        dens = dot3(c_hi[rows, :], c_lo[rows, :], c_hi[cols, :], c_lo[cols, :]) * scale
        for k in range(4):
            for q in range(NX):
                start = k * 64 + q * 16
                dbuf[k % 2, q, ra * 2 + k // 2, :, cols] = dens[start:start + 16]
        return carry

    lax.fori_loop(0, 4, dens_tile, 0)

    core_copies = []
    for d in (1, 2, 3, 0):
        q = (x + d) % NX
        copy = remote(dbuf.at[1 - c, q], dpart.at[q], c_s.at[d], c_r.at[d], w, 2 * y + 1 - c)
        copy.start()
        core_copies.append(copy)
    x_copies = []
    for copy, d in zip(core_copies, (1, 2, 3, 0)):
        q = (x + d) % NX
        copy.wait_recv()
        s0[q] = dbuf[c, q] + dpart[q]
        if d:
            out = remote(s0.at[q], xbuf.at[d], xs_s.at[d], xs_r.at[d], at_x(d), n)
            out.start()
            x_copies.append(out)
    for copy in x_copies:
        copy.wait_recv()
    sum_x = ((s0[x] + xbuf[1]) + xbuf[2]) + xbuf[3]
    for k in range(NZ):
        r, q = k // 4, k % 4
        s1[k] = sum_x[:, r * 8:r * 8 + 8, q * 128:q * 128 + 128]

    z_copies = []
    for d in range(1, NZ):
        copy = remote(s1.at[(z + d) % NZ], zbuf.at[d], zs_s.at[d], zs_r.at[d], at_z(d), n)
        copy.start()
        z_copies.append(copy)
    for copy in z_copies:
        copy.wait_recv()
    sum_z = s1[z]
    for d in range(1, NZ):
        sum_z = sum_z + zbuf[d]
    s2[...] = sum_z

    y_copies = []
    for d in range(1, 2 * NY):
        wide, narrow = at_y(d)
        copy = remote(s2.at[(y + d) % NY], ybuf.at[gy], ys_s.at[d], ys_r.at[d], wide, narrow)
        copy.start()
        y_copies.append(copy)
    ybuf[gy] = s2[y]
    for copy in y_copies:
        copy.wait_recv()
    sum_y = ybuf[0]
    for k in range(1, 2 * NY):
        sum_y = sum_y + ybuf[k]
    tbuf[...] = sum_y

    rows = pl.ds(pl.multiple_of(x * 16 + (z // 4) * 8, 8), 8)
    cols = pl.ds(pl.multiple_of((z % 4) * 128, 128), 128)
    gz = []
    for d in range(1, NZ):
        copy = remote(tbuf, ofull.at[rows, cols], gz_s.at[d], gz_r.at[d], at_z(d), n)
        copy.start()
        gz.append(copy)
    ofull[rows, cols] = sum_y
    for copy in gz:
        copy.wait_recv()
    rows = pl.ds(pl.multiple_of(x * 16, 16), 16)
    gx = []
    for d in range(1, NX):
        copy = remote(ofull.at[rows], ofull.at[rows], gx_s.at[d], gx_r.at[d], at_x(d), n)
        copy.start()
        gx.append(copy)
    pv_copy.wait()
    energy_out[...] = pv_own[...] + pv_in[...]
    for copy in gx:
        copy.wait_recv()
    dens_out[...] = ofull[...]

    for copy in m1 + m2 + m3 + a2a[1:] + forwards + core_copies + x_copies + z_copies + y_copies + gz + gx:
        copy.wait_send()


def on_device(n_wide, raw_ints, metric, occ_energy, vir_energy, pair_kept):
    orbitals, vir_local, aux = raw_ints.shape
    virtuals = vir_energy.shape[0]
    dens_scale = 0.0625 / (n_wide * NARROW)
    side = jnp.stack([occ_energy, pair_kept.astype(F32)])[:, :, None]
    side = jnp.broadcast_to(side, (2, 8, 128))
    dma = pltpu.SemaphoreType.DMA
    vmem = pltpu.VMEM
    fit_shape = (orbitals, vir_local, aux)
    scratch = [
        vmem(fit_shape, F32), vmem(fit_shape, F32), vmem((aux, aux), F32),
        vmem((aux, aux), BF16), vmem((aux, aux), BF16),
        vmem((256, aux), BF16), vmem((256, aux), BF16),
        vmem(fit_shape, BF16), vmem(fit_shape, BF16), vmem(fit_shape, BF16), vmem(fit_shape, BF16),
        vmem((virtuals, virtuals), F32), vmem((virtuals, virtuals), F32), vmem((virtuals, virtuals), F32),
        vmem((virtuals, 2 * virtuals), BF16), vmem((virtuals, 2 * virtuals), BF16),
        vmem((2, NX, NY, 16, virtuals), F32), vmem((NX, NY, 16, virtuals), F32), vmem((NX, NY, 16, virtuals), F32),
        vmem((NX, NY, 16, virtuals), F32),
        vmem((NZ, NY, 8, 128), F32), vmem((NZ, NY, 8, 128), F32), vmem((NY, 8, 128), F32),
        vmem((2 * NY, 8, 128), F32), vmem((8, 128), F32), vmem((vir_local, virtuals), F32),
        vmem((2, 8, 128), F32), vmem((8, 128), F32), vmem((8, 128), F32),
        dma((2,)), dma((8,)), dma((8,)), dma((8,)), dma((8,)),
        dma((4,)), dma((4,)), dma((4,)), dma((4,)), dma((4,)), dma((4,)), dma((2,)), dma((2,)),
        dma((4,)), dma((4,)), dma((4,)), dma((4,)), dma((8,)), dma((8,)), dma((8,)), dma((8,)),
        dma((8,)), dma((8,)), dma((4,)), dma((4,)),
    ]
    any_space = pl.BlockSpec(memory_space=pl.ANY)
    in_vmem = pl.BlockSpec(memory_space=pltpu.VMEM)
    density, energy = pl.pallas_call(
        functools.partial(kernel, n_wide, dens_scale),
        out_shape=(
            jax.ShapeDtypeStruct((vir_local, virtuals), F32),
            jax.ShapeDtypeStruct((8, 128), F32),
        ),
        in_specs=[any_space, any_space, in_vmem, in_vmem],
        out_specs=(in_vmem, in_vmem),
        scratch_shapes=scratch,
        compiler_params=pltpu.CompilerParams(
            collective_id=0, has_side_effects=True, vmem_limit_bytes=48 << 20
        ),
        name="pair_density",
    )(raw_ints, metric, side, vir_energy[None, :])
    return density, energy[0, :1]


def solution(mesh):
    placed = (
        P("wide", "narrow", None),
        P("narrow", None),
        P(("wide", "narrow")),
        P(),
        P(("wide", "narrow")),
    )
    return jax.shard_map(
        functools.partial(on_device, mesh.shape["wide"]),
        mesh=mesh,
        in_specs=placed,
        out_specs=(P("narrow", None), P(("wide", "narrow"))),
        check_vma=False,
    )
```

```python
import functools

import jax
import jax.numpy as jnp
from jax import lax
from jax.experimental import pallas as pl
from jax.experimental.pallas import tpu as pltpu
from jax.sharding import PartitionSpec as P

MESH = pl.DeviceIdType.MESH
F32 = jnp.float32
BF16 = jnp.bfloat16

NX, NZ, NY, NARROW = 4, 8, 4, 8
PLANE = NX * NZ
LAST, FIRST = PLANE - 1, 0
UP_COLUMNS = (24, 7, 25, 6)
DOWN_COLUMNS = (23, 8, 16, 15)


def split(value):
    high = value.astype(BF16)
    return high, (value - high.astype(F32)).astype(BF16)


def dot_nt(left, right):
    return lax.dot_general(left, right, (((1,), (1,)), ((), ())), preferred_element_type=F32)


def dot3(left_hi, left_lo, right_hi, right_lo):
    return dot_nt(left_hi, right_hi) + (dot_nt(left_hi, right_lo) + dot_nt(left_lo, right_hi))


def kernel(
    n_wide, dens_scale,
    raw, metric, side, vir,
    dens_out, energy_out,
    rbuf, jbuf, mbuf, m_hi, m_lo, x_hi, x_lo, fi_hi, fi_lo, fj_hi, fj_lo,
    rinv, pbuf, abuf, c_hi, c_lo, dbuf, dpart, s0, xbuf, s1, zbuf, s2, ybuf, tbuf, ofull,
    side_in, pv_own, pv_in,
    relay_buf, b_s, b_r, r_s,
    loc_sem, a_s, a_r, f_s, f_r, m1_s, m1_r, m2_s, m2_r, m3_s, m3_r, side_sem, pv_sem,
    c_s, c_r, xs_s, xs_r, zs_s, zs_r, ys_s, ys_r, gz_s, gz_r, gx_s, gx_r,
):
    w = lax.axis_index("wide")
    n = lax.axis_index("narrow")
    y, c = n // 2, n % 2
    hi, plane = w // PLANE, w % PLANE
    x, z = plane // NZ, plane % NZ
    gy = hi * NY + y
    up = (w + 1) % n_wide
    down = (w + n_wide - 1) % n_wide
    fwd = (w + 1 - 2 * c + n_wide) % n_wide
    back = (w - 1 + 2 * c + n_wide) % n_wide

    def remote(src, dst, ss, rs, wide, narrow):
        return pltpu.make_async_remote_copy(
            src_ref=src, dst_ref=dst, send_sem=ss, recv_sem=rs,
            device_id=(wide, narrow), device_id_type=MESH,
        )

    def at_x(d):
        return hi * PLANE + ((x + d) % NX) * NZ + z

    def at_z(d):
        return hi * PLANE + x * NZ + (z + d) % NZ

    def at_y(d):
        there = (gy + d) % (2 * NY)
        return (there // NY) * PLANE + plane, 2 * (there % NY) + c

    peers = [(w, (n + d) % NARROW) for d in range(1, NARROW)]
    peers += [at_y(d) for d in range(1, 2 * NY)]
    peers += [(at_x(d), n) for d in range(1, NX)]
    peers += [(at_z(d), n) for d in range(1, NZ)]
    peers += [(up, n), (down, n)]
    barrier = pltpu.get_barrier_semaphore()

    def greet(wide, narrow):
        pl.semaphore_signal(barrier, inc=1, device_id=(wide, narrow), device_id_type=MESH)

    for peer in peers:
        greet(*peer)
    routes = ((LAST, FIRST, 0, UP_COLUMNS), (FIRST, LAST, 1, DOWN_COLUMNS))
    sends_on = jnp.logical_not(((plane == LAST) & (c == 0)) | ((plane == FIRST) & (c == 1)))
    for source, target, parity, columns in routes:
        @pl.when(plane == source)
        def _():
            for column in columns:
                greet(hi * PLANE + column, n)

        for j, column in enumerate(columns):
            @pl.when(plane == column)
            def _():
                greet(hi * PLANE + source, n)
                greet((1 - hi) * PLANE + target, 2 * ((j + NY - y) % NY) + parity)

        @pl.when((plane == target) & (c == parity))
        def _():
            for j, column in enumerate(columns):
                for core in range(2):
                    greet((1 - hi) * PLANE + column, 2 * ((j + NY - y) % NY) + core)

    at_end = (plane == LAST) | (plane == FIRST)
    on_way = plane == UP_COLUMNS[0]
    for column in UP_COLUMNS[1:] + DOWN_COLUMNS:
        on_way = on_way | (plane == column)
    for case, more in (
        (at_end & sends_on, 3 * len(UP_COLUMNS)),
        (at_end & jnp.logical_not(sends_on), len(UP_COLUMNS)),
        (on_way, 2),
        (jnp.logical_not(at_end | on_way), 0),
    ):
        @pl.when(case)
        def _():
            pl.semaphore_wait(barrier, len(peers) + more)

    rows_q = metric.shape[0] // NX
    own_rows = pl.ds(x * (NY * rows_q) + y * rows_q, rows_q)
    m1 = []
    for d in range(1, NY):
        copy = remote(
            metric.at[pl.ds(x * rows_q, rows_q)], mbuf.at[own_rows],
            m1_s.at[d], m1_r.at[d], w, 2 * ((y + d) % NY) + c,
        )
        copy.start()
        m1.append(copy)
    m_local = pltpu.make_async_copy(metric.at[pl.ds(x * rows_q, rows_q)], mbuf.at[own_rows], loc_sem.at[0])
    m_local.start()
    side_copy = remote(side, side_in, side_sem.at[0], side_sem.at[1], fwd, n)
    side_copy.start()

    for source, target, parity, columns in routes:
        @pl.when(plane == source)
        def _():
            for j, column in enumerate(columns):
                k = (j + NY - y) % NY
                remote(
                    raw.at[2 * k + parity], relay_buf, b_s.at[j], b_r.at[0], hi * PLANE + column, n
                ).start()

    a2a = [None]
    for d in range(1, NARROW):
        to = (n + d) % NARROW
        copy = remote(raw.at[to], rbuf.at[n], a_s.at[d], a_r.at[d], w, to)
        copy.start()
        a2a.append(copy)
    own_slot = pltpu.make_async_copy(raw.at[n], rbuf.at[n], loc_sem.at[1])
    own_slot.start()
    slots = [(n + NARROW - d) % NARROW for d in range(NARROW)]
    forwards = []

    def forward(d):
        src = raw.at[n] if d == 0 else rbuf.at[slots[d]]
        copy = remote(src, jbuf.at[slots[d]], f_s.at[d], f_r.at[d], fwd, n)
        forwards.append(copy)

        @pl.when(sends_on)
        def _():
            copy.start()

    forward(0)
    a2a[1].wait_recv()
    forward(1)

    def second_leg(target, parity, j):
        to = 2 * ((j + NY - y) % NY) + parity
        return remote(
            relay_buf, jbuf.at[n], r_s.at[0], f_r.at[(to + NARROW - n) % NARROW], (1 - hi) * PLANE + target, to
        )

    for source, target, parity, columns in routes:
        for j, column in enumerate(columns):
            @pl.when(plane == column)
            def _():
                remote(raw.at[0], relay_buf, b_s.at[j], b_r.at[0], hi * PLANE + source, n).wait_recv()
                second_leg(target, parity, j).start()

    m_local.wait()
    for copy in m1:
        copy.wait_recv()
    block = NY * rows_q
    half = NX * block
    m2 = []
    for d in range(1, NX):
        rows = pl.ds(x * block, block)
        copy = remote(mbuf.at[rows], mbuf.at[rows], m2_s.at[d], m2_r.at[d], at_x(d), n)
        copy.start()
        m2.append(copy)
    m3 = []

    def to_partner(d):
        which = (x + NX - d) % NX
        copy = remote(
            mbuf.at[pl.ds(which * block, block)], mbuf.at[pl.ds(half + which * block, block)],
            m3_s.at[d], m3_r.at[d], w, 2 * y + 1 - c,
        )
        copy.start()
        m3.append(copy)

    to_partner(0)

    side_copy.wait()
    virtuals = vir.shape[1]
    rinv[...] = jnp.broadcast_to(vir[...], (virtuals, virtuals))
    energies = side[0][:1, :1] + side_in[0][:1, :1]
    for r in range(0, virtuals, 128):
        across = rinv[:, r:r + 128].T
        pbuf[r:r + 128, :] = 1.0 / ((rinv[r:r + 128, :] + across) - energies)

    for d in (2, 3, 4):
        a2a[d].wait_recv()
        forward(d)
    for d in range(1, NX):
        m2[d - 1].wait_recv()
        to_partner(d)
    a2a[5].wait_recv()
    forward(5)
    for copy in m3:
        copy.wait_recv()

    def split_rows(k, carry):
        rows = pl.ds(pl.multiple_of(k * 96, 96), 96)
        m_hi[rows, :], m_lo[rows, :] = split(mbuf[rows, :])
        return carry

    lax.fori_loop(0, mbuf.shape[0] // 96, split_rows, 0)

    def fit(src, f_hi, f_lo, four):
        for k, slot in enumerate(four):
            part = pl.ds(k * 64, 64)
            x_hi[part, :], x_lo[part, :] = split(src[slot])

        def tile(t, carry):
            cols = pl.ds(pl.multiple_of(t * 256, 256), 256)
            fitted = dot3(x_hi[...], x_lo[...], m_hi[cols, :], m_lo[cols, :])
            high, low = split(fitted)
            for k, slot in enumerate(four):
                f_hi[slot, :, cols] = high[k * 64:(k + 1) * 64]
                f_lo[slot, :, cols] = low[k * 64:(k + 1) * 64]
            return carry

        lax.fori_loop(0, mbuf.shape[0] // 256, tile, 0)

    for d in (6, 7):
        a2a[d].wait_recv()
        forward(d)
    own_slot.wait()
    fit(rbuf, fi_hi, fi_lo, slots[:4])
    fit(rbuf, fi_hi, fi_lo, slots[4:])
    for d in range(4):
        forwards[d].wait_recv()
    fit(jbuf, fj_hi, fj_lo, slots[:4])
    for d in range(4, 8):
        forwards[d].wait_recv()
    fit(jbuf, fj_hi, fj_lo, slots[4:])

    rinv[...] = pbuf[...]

    def pair_tile(t, carry):
        ra, cb = t // 2, t % 2
        four_a, four_b = pl.ds(ra * 4, 4), pl.ds(cb * 4, 4)
        shape = (256, fi_hi.shape[2])
        ints = dot3(
            fi_hi[four_a].reshape(shape), fi_lo[four_a].reshape(shape),
            fj_hi[four_b].reshape(shape), fj_lo[four_b].reshape(shape),
        )
        rows = pl.ds(pl.multiple_of(ra * 256, 256), 256)
        cols = pl.ds(pl.multiple_of(cb * 256, 256), 256)
        pbuf[rows, cols] = ints
        abuf[rows, cols] = ints * rinv[rows, cols]
        return carry

    lax.fori_loop(0, 4, pair_tile, 0)

    def value_tile(t, total):
        ra, cb = t // 2, t % 2
        rows = pl.ds(pl.multiple_of(ra * 256, 256), 256)
        cols = pl.ds(pl.multiple_of(cb * 256, 256), 256)
        cols_t = pl.ds(pl.multiple_of(virtuals + cb * 256, 256), 256)
        amp = abuf[rows, cols]
        amp_t = abuf[cols, rows].T
        c_hi[rows, cols], c_lo[rows, cols] = split(amp)
        c_hi[rows, cols_t], c_lo[rows, cols_t] = split(amp_t)
        return total + jnp.sum(pbuf[rows, cols] * (2.0 * amp - amp_t), axis=0, keepdims=True)

    total = lax.fori_loop(0, 4, value_tile, jnp.zeros((1, 256), F32))
    kept = jnp.where(c == 0, side[1], side_in[1])
    pair_sum = jnp.sum(total, axis=1, keepdims=True)
    pv_own[...] = -kept * (jnp.broadcast_to(pair_sum, kept.shape) / (virtuals * virtuals))
    pv_copy = remote(pv_own, pv_in, pv_sem.at[0], pv_sem.at[1], back, n)
    pv_copy.start()

    scale = kept[:1, :1] * dens_scale

    core_copies = [None] * NX
    quarters = [((x // 2 + 1 + d // 2) % 2) * 2 + (x + d + d // 2) % 2 for d in range(NX)]
    for d in range(NX):
        q = quarters[d]
        if d % 2 == 0:
            half_cols = q // 2

            def dens_tile(ra, carry):
                rows = pl.ds(pl.multiple_of(ra * 256, 256), 256)
                cols = pl.ds(pl.multiple_of(half_cols * 256, 256), 256)
                dens = dot3(c_hi[rows, :], c_lo[rows, :], c_hi[cols, :], c_lo[cols, :]) * scale
                for k in range(4):
                    for e in range(2):
                        dbuf[half_cols * 2 + e, k % 2, ra * 2 + k // 2] = dens[k * 64:k * 64 + 64, e * 128:e * 128 + 128]
                return carry

            lax.fori_loop(0, 2, dens_tile, 0)
        copy = remote(dbuf.at[q, 1 - c], dpart.at[q], c_s.at[d], c_r.at[d], w, 2 * y + 1 - c)
        copy.start()
        core_copies[d] = copy
    x_copies = []
    for copy, d in zip(core_copies, range(NX)):
        q = quarters[d]
        copy.wait_recv()
        s0[q] = dbuf[q, c] + dpart[q]
        if d < NX - 1:
            out = remote(s0.at[q], xbuf.at[x], xs_s.at[d], xs_r.at[d], hi * PLANE + q * NZ + z, n)
            out.start()
            x_copies.append(out)
    for copy in x_copies:
        copy.wait_recv()
    xbuf[x] = s0[x]
    sum_x = ((xbuf[0] + xbuf[1]) + xbuf[2]) + xbuf[3]
    for k in range(NZ):
        s1[k] = sum_x[:, k * 8:k * 8 + 8, :]

    z_copies = []
    for d in range(1, NZ):
        copy = remote(s1.at[(z + d) % NZ], zbuf.at[d], zs_s.at[d], zs_r.at[d], at_z(d), n)
        copy.start()
        z_copies.append(copy)
    for copy in z_copies:
        copy.wait_recv()
    sum_z = s1[z]
    for d in range(1, NZ):
        sum_z = sum_z + zbuf[d]
    s2[...] = sum_z

    y_copies = []
    for d in range(1, 2 * NY):
        wide, narrow = at_y(d)
        copy = remote(s2.at[(y + d) % NY], ybuf.at[gy], ys_s.at[d], ys_r.at[d], wide, narrow)
        copy.start()
        y_copies.append(copy)
    ybuf[gy] = s2[y]
    for copy in y_copies:
        copy.wait_recv()
    sum_y = ybuf[0]
    for k in range(1, 2 * NY):
        sum_y = sum_y + ybuf[k]
    tbuf[...] = sum_y

    rows = pl.ds(pl.multiple_of(z * 8, 8), 8)
    cols = pl.ds(pl.multiple_of(x * 128, 128), 128)
    gz = []
    for d in range(1, NZ):
        copy = remote(tbuf, ofull.at[rows, cols], gz_s.at[d], gz_r.at[d], at_z(d), n)
        copy.start()
        gz.append(copy)
    ofull[rows, cols] = sum_y
    for copy in gz:
        copy.wait_recv()
    gx = []
    for d in range(1, NX):
        copy = remote(ofull.at[:, cols], ofull.at[:, cols], gx_s.at[d], gx_r.at[d], at_x(d), n)
        copy.start()
        gx.append(copy)
    pv_copy.wait()
    energy_out[...] = pv_own[...] + pv_in[...]
    for copy in gx:
        copy.wait_recv()
    dens_out[...] = ofull[...]

    for source, target, parity, columns in routes:
        @pl.when(plane == source)
        def _():
            for j, column in enumerate(columns):
                remote(raw.at[0], relay_buf, b_s.at[j], b_r.at[0], hi * PLANE + column, n).wait_send()

        for j, column in enumerate(columns):
            @pl.when(plane == column)
            def _():
                second_leg(target, parity, j).wait_send()

    @pl.when(sends_on)
    def _():
        for copy in forwards:
            copy.wait_send()

    for copy in m1 + m2 + m3 + a2a[1:] + core_copies + x_copies + z_copies + y_copies + gz + gx:
        copy.wait_send()


def on_device(n_wide, raw_ints, metric, occ_energy, vir_energy, pair_kept):
    orbitals, vir_local, aux = raw_ints.shape
    virtuals = vir_energy.shape[0]
    dens_scale = 0.0625 / (n_wide * NARROW)
    side = jnp.stack([occ_energy, pair_kept.astype(F32)])[:, :, None]
    side = jnp.broadcast_to(side, (2, 8, 128))
    dma = pltpu.SemaphoreType.DMA
    vmem = pltpu.VMEM
    fit_shape = (orbitals, vir_local, aux)
    scratch = [
        vmem(fit_shape, F32), vmem(fit_shape, F32), vmem((aux, aux), F32),
        vmem((aux, aux), BF16), vmem((aux, aux), BF16),
        vmem((256, aux), BF16), vmem((256, aux), BF16),
        vmem(fit_shape, BF16), vmem(fit_shape, BF16), vmem(fit_shape, BF16), vmem(fit_shape, BF16),
        vmem((virtuals, virtuals), F32), vmem((virtuals, virtuals), F32), vmem((virtuals, virtuals), F32),
        vmem((virtuals, 2 * virtuals), BF16), vmem((virtuals, 2 * virtuals), BF16),
        vmem((NX, 2, NY, 64, 128), F32), vmem((NX, NY, 64, 128), F32), vmem((NX, NY, 64, 128), F32),
        vmem((NX, NY, 64, 128), F32),
        vmem((NZ, NY, 8, 128), F32), vmem((NZ, NY, 8, 128), F32), vmem((NY, 8, 128), F32),
        vmem((2 * NY, 8, 128), F32), vmem((8, 128), F32), vmem((vir_local, virtuals), F32),
        vmem((2, 8, 128), F32), vmem((8, 128), F32), vmem((8, 128), F32),
        vmem((vir_local, aux), F32), dma((4,)), dma((1,)), dma((1,)),
        dma((2,)), dma((8,)), dma((8,)), dma((8,)), dma((8,)),
        dma((4,)), dma((4,)), dma((4,)), dma((4,)), dma((4,)), dma((4,)), dma((2,)), dma((2,)),
        dma((4,)), dma((4,)), dma((4,)), dma((4,)), dma((8,)), dma((8,)), dma((8,)), dma((8,)),
        dma((8,)), dma((8,)), dma((4,)), dma((4,)),
    ]
    in_hbm = pl.BlockSpec(memory_space=pltpu.HBM)
    in_vmem = pl.BlockSpec(memory_space=pltpu.VMEM)
    density, energy = pl.pallas_call(
        functools.partial(kernel, n_wide, dens_scale),
        out_shape=(
            jax.ShapeDtypeStruct((vir_local, virtuals), F32),
            jax.ShapeDtypeStruct((8, 128), F32),
        ),
        in_specs=[in_hbm, in_hbm, in_vmem, in_vmem],
        out_specs=(in_vmem, in_vmem),
        scratch_shapes=scratch,
        compiler_params=pltpu.CompilerParams(
            collective_id=0, has_side_effects=True, vmem_limit_bytes=48 << 20
        ),
        name="pair_density",
    )(raw_ints, metric, side, vir_energy[None, :])
    return density, energy[0, :1]


def solution(mesh):
    placed = (
        P("wide", "narrow", None),
        P("narrow", None),
        P(("wide", "narrow")),
        P(),
        P(("wide", "narrow")),
    )
    return jax.shard_map(
        functools.partial(on_device, mesh.shape["wide"]),
        mesh=mesh,
        in_specs=placed,
        out_specs=(P("narrow", None), P(("wide", "narrow"))),
        check_vma=False,
    )
```

```python
import functools

import jax
import jax.numpy as jnp
from jax import lax
from jax.experimental import pallas as pl
from jax.experimental.pallas import tpu as pltpu
from jax.sharding import PartitionSpec as P

MESH = pl.DeviceIdType.MESH
F32 = jnp.float32
BF16 = jnp.bfloat16

NX, NZ, NY, NARROW = 4, 8, 4, 8
PLANE = NX * NZ
LAST, FIRST = PLANE - 1, 0
UP_COLUMNS = ((24, 3, None), (6, 1, 0), (30, 1, 1), (26, 0, 0), (2, 0, 1), (4, 2, 0), (28, 2, 1))
DOWN_COLUMNS = tuple((LAST - column, j, core) for column, j, core in UP_COLUMNS)


def split(value):
    high = value.astype(BF16)
    return high, (value - high.astype(F32)).astype(BF16)


def dot_nt(left, right):
    return lax.dot_general(left, right, (((1,), (1,)), ((), ())), preferred_element_type=F32)


def dot3(left_hi, left_lo, right_hi, right_lo):
    return dot_nt(left_hi, right_hi) + (dot_nt(left_hi, right_lo) + dot_nt(left_lo, right_hi))


def kernel(
    n_wide, dens_scale,
    raw, metric, side, vir,
    dens_out, energy_out,
    rbuf, jbuf, mbuf, m_hi, m_lo, x_hi, x_lo, fi_hi, fi_lo, fj_hi, fj_lo,
    rinv, pbuf, abuf, c_hi, c_lo, dbuf, dpart, s0, xbuf, s1, zbuf, s2, ybuf, tbuf, ofull,
    side_in, pv_own, pv_in,
    relay_buf, b_s, b_r, r_s,
    loc_sem, a_s, a_r, f_s, f_r, m1_s, m1_r, m2_s, m2_r, m3_s, m3_r, side_sem, pv_sem,
    c_s, c_r, xs_s, xs_r, zs_s, zs_r, ys_s, ys_r, gz_s, gz_r,
):
    w = lax.axis_index("wide")
    n = lax.axis_index("narrow")
    y, c = n // 2, n % 2
    hi, plane = w // PLANE, w % PLANE
    x, z = plane // NZ, plane % NZ
    gy = hi * NY + y
    up = (w + 1) % n_wide
    down = (w + n_wide - 1) % n_wide
    fwd = (w + 1 - 2 * c + n_wide) % n_wide
    back = (w - 1 + 2 * c + n_wide) % n_wide

    def remote(src, dst, ss, rs, wide, narrow):
        return pltpu.make_async_remote_copy(
            src_ref=src, dst_ref=dst, send_sem=ss, recv_sem=rs,
            device_id=(wide, narrow), device_id_type=MESH,
        )

    def at_x(d):
        return hi * PLANE + ((x + d) % NX) * NZ + z

    def at_z(d):
        return hi * PLANE + x * NZ + (z + d) % NZ

    def at_y(d):
        there = (gy + d) % (2 * NY)
        return (there // NY) * PLANE + plane, 2 * (there % NY) + c

    peers = [(w, (n + d) % NARROW) for d in range(1, NARROW)]
    peers += [at_y(d) for d in range(1, 2 * NY)]
    peers += [
        (hi * PLANE + ((x + d // NZ) % NX) * NZ + (z + d % NZ) % NZ, n) for d in range(1, PLANE)
    ]
    peers += [(up, n), (down, n)]
    barrier = pltpu.get_barrier_semaphore()

    def greet(wide, narrow):
        pl.semaphore_signal(barrier, inc=1, device_id=(wide, narrow), device_id_type=MESH)

    for peer in peers:
        greet(*peer)
    routes = ((LAST, FIRST, 0, UP_COLUMNS), (FIRST, LAST, 1, DOWN_COLUMNS))
    sends_on = jnp.logical_not(((plane == LAST) & (c == 0)) | ((plane == FIRST) & (c == 1)))
    def takes(core):
        return c == c if core is None else c == core

    for source, target, parity, columns in routes:
        for column, j, core in columns:
            @pl.when((plane == source) & takes(core))
            def _():
                greet(hi * PLANE + column, n)

            @pl.when((plane == column) & takes(core))
            def _():
                greet(hi * PLANE + source, n)
                greet((1 - hi) * PLANE + target, 2 * ((j + NY - y) % NY) + parity)

            @pl.when((plane == target) & (c == parity))
            def _():
                for from_core in (0, 1) if core is None else (core,):
                    greet((1 - hi) * PLANE + column, 2 * ((j + NY - y) % NY) + from_core)

    at_end = (plane == LAST) | (plane == FIRST)
    on_way = plane < 0
    for column, j, core in UP_COLUMNS + DOWN_COLUMNS:
        on_way = on_way | ((plane == column) & takes(core))
    for case, more in (
        (at_end & sends_on, NY + NARROW),
        (at_end & jnp.logical_not(sends_on), NY),
        (on_way, 2),
        (jnp.logical_not(at_end | on_way), 0),
    ):
        @pl.when(case)
        def _():
            pl.semaphore_wait(barrier, len(peers) + more)

    rows_q = metric.shape[0] // NX
    half_aux = metric.shape[1] // 2
    block = NY * rows_q
    half = NX * block
    mine = z % 2

    def aux_half(piece):
        return pl.ds(pl.multiple_of(piece * half_aux, half_aux), half_aux)

    share = metric.at[pl.ds(x * rows_q, rows_q), aux_half(mine)]
    own_part = mbuf.at[pl.ds(x * block + y * rows_q, rows_q), aux_half(mine)]
    m1 = []
    for d in range(1, NY):
        copy = remote(share, own_part, m1_s.at[d], m1_r.at[d], w, 2 * ((y + d) % NY) + c)
        copy.start()
        m1.append(copy)
    m_local = pltpu.make_async_copy(share, own_part, loc_sem.at[0])
    m_local.start()
    side_copy = remote(side, side_in, side_sem.at[0], side_sem.at[1], fwd, n)
    side_copy.start()

    for source, target, parity, columns in routes:
        for column, j, core in columns:
            @pl.when((plane == source) & takes(core))
            def _():
                k = (j + NY - y) % NY
                remote(
                    raw.at[2 * k + parity], relay_buf, b_s.at[j], b_r.at[0], hi * PLANE + column, n
                ).start()

    a2a = [None]
    for d in range(1, NARROW):
        to = (n + d) % NARROW
        copy = remote(raw.at[to], rbuf.at[n], a_s.at[d], a_r.at[d], w, to)
        copy.start()
        a2a.append(copy)
    own_slot = pltpu.make_async_copy(raw.at[n], rbuf.at[n], loc_sem.at[1])
    own_slot.start()
    slots = [(n + NARROW - d) % NARROW for d in range(NARROW)]
    forwards = []

    def forward(d):
        src = raw.at[n] if d == 0 else rbuf.at[slots[d]]
        copy = remote(src, jbuf.at[slots[d]], f_s.at[d], f_r.at[d], fwd, n)
        forwards.append(copy)

        @pl.when(sends_on)
        def _():
            copy.start()

    forward(0)
    a2a[1].wait_recv()
    forward(1)

    def second_leg(target, parity, j):
        to = 2 * ((j + NY - y) % NY) + parity
        return remote(
            relay_buf, jbuf.at[n], r_s.at[0], f_r.at[(to + NARROW - n) % NARROW], (1 - hi) * PLANE + target, to
        )

    for source, target, parity, columns in routes:
        for column, j, core in columns:
            @pl.when((plane == column) & takes(core))
            def _():
                remote(raw.at[0], relay_buf, b_s.at[j], b_r.at[0], hi * PLANE + source, n).wait_recv()
                second_leg(target, parity, j).start()

    m_local.wait()
    for copy in m1:
        copy.wait_recv()

    def m_piece(which, piece):
        return mbuf.at[pl.ds(which * block, block), aux_half(piece)]

    def around_x(way, piece):
        src = m_piece(x, piece)
        k = 2 * way + piece
        return remote(src, src, m2_s.at[k], m2_r.at[k], at_x(1 - 2 * way + NX), n)

    def on_around_x(way):
        src = m_piece((x + NX - 1 + 2 * way) % NX, way)
        return remote(src, src, m2_s.at[4 + way], m2_r.at[4 + way], at_x(1 - 2 * way + NX), n)

    m_z = remote(
        m_piece(x, mine), m_piece(x, mine), m1_s.at[0], m1_r.at[0], hi * PLANE + x * NZ + z + 1 - 2 * mine, n
    )
    m_z.start()
    for way in (0, 1):
        around_x(way, mine).start()
    m3 = []

    def to_partner(d):
        which = (x + d) % NX
        copy = remote(
            mbuf.at[pl.ds(which * block, block)], mbuf.at[pl.ds(half + which * block, block)],
            m3_s.at[d], m3_r.at[d], w, 2 * y + 1 - c,
        )
        copy.start()
        m3.append(copy)

    side_copy.wait()
    virtuals = vir.shape[1]
    pbuf[...] = jnp.broadcast_to(vir[...], (virtuals, virtuals))
    energies = side[0][:1, :1] + side_in[0][:1, :1]
    for r in range(0, virtuals, 128):
        across = pbuf[:, r:r + 128].T
        rinv[r:r + 128, :] = 1.0 / ((pbuf[r:r + 128, :] + across) - energies)

    m_z.wait_recv()
    for way in (0, 1):
        around_x(way, 1 - mine).start()
    to_partner(0)
    for d in (2, 3):
        a2a[d].wait_recv()
        forward(d)
    for way in (0, 1):
        around_x(way, way).wait_recv()
        on_around_x(way).start()
    a2a[4].wait_recv()
    forward(4)
    for way in (0, 1):
        around_x(way, 1 - way).wait_recv()
        to_partner(3 - 2 * way)
    for way in (0, 1):
        on_around_x(way).wait_recv()
    to_partner(2)
    a2a[5].wait_recv()
    forward(5)
    for copy in m3:
        copy.wait_recv()

    def split_rows(k, carry):
        rows = pl.ds(pl.multiple_of(k * 96, 96), 96)
        m_hi[rows, :], m_lo[rows, :] = split(mbuf[rows, :])
        return carry

    lax.fori_loop(0, mbuf.shape[0] // 96, split_rows, 0)

    def fit(src, f_hi, f_lo, four):
        for k, slot in enumerate(four):
            part = pl.ds(k * 64, 64)
            x_hi[part, :], x_lo[part, :] = split(src[slot])

        def tile(t, carry):
            cols = pl.ds(pl.multiple_of(t * 256, 256), 256)
            fitted = dot3(x_hi[...], x_lo[...], m_hi[cols, :], m_lo[cols, :])
            high, low = split(fitted)
            for k, slot in enumerate(four):
                f_hi[slot, :, cols] = high[k * 64:(k + 1) * 64]
                f_lo[slot, :, cols] = low[k * 64:(k + 1) * 64]
            return carry

        lax.fori_loop(0, mbuf.shape[0] // 256, tile, 0)

    own_slot.wait()
    fit(rbuf, fi_hi, fi_lo, slots[:4])
    a2a[6].wait_recv()
    forward(6)
    for d in range(4):
        forwards[d].wait_recv()
    fit(jbuf, fj_hi, fj_lo, slots[:4])
    a2a[7].wait_recv()
    forward(7)
    fit(rbuf, fi_hi, fi_lo, slots[4:])

    def pair_rows(four):
        for k, slot in enumerate(four):
            part = pl.ds(k * 64, 64)
            x_hi[part, :] = fj_hi[slot]
            x_lo[part, :] = fj_lo[slot]

        def tile(cb, carry):
            four_b = pl.ds(cb * 4, 4)
            shape = (256, fi_hi.shape[2])
            ints = dot3(x_hi[...], x_lo[...], fi_hi[four_b].reshape(shape), fi_lo[four_b].reshape(shape))
            cols = pl.ds(pl.multiple_of(cb * 256, 256), 256)
            for k, slot in enumerate(four):
                rows = pl.ds(pl.multiple_of(slot * 64, 64), 64)
                part = ints[k * 64:(k + 1) * 64]
                pbuf[rows, cols] = part
                abuf[rows, cols] = part * rinv[rows, cols]
            return carry

        lax.fori_loop(0, 2, tile, 0)

    pair_rows(slots[:4])
    for d in range(4, 8):
        forwards[d].wait_recv()
    fit(jbuf, fj_hi, fj_lo, slots[4:])
    pair_rows(slots[4:])

    def value_tile(t, total):
        ra, cb = t // 2, t % 2
        rows = pl.ds(pl.multiple_of(ra * 256, 256), 256)
        cols = pl.ds(pl.multiple_of(cb * 256, 256), 256)
        cols_t = pl.ds(pl.multiple_of(virtuals + cb * 256, 256), 256)
        amp = abuf[rows, cols]
        amp_t = abuf[cols, rows].T
        c_hi[rows, cols], c_lo[rows, cols] = split(amp)
        c_hi[rows, cols_t], c_lo[rows, cols_t] = split(amp_t)
        return total + jnp.sum(pbuf[rows, cols] * (2.0 * amp - amp_t), axis=0, keepdims=True)

    total = lax.fori_loop(0, 4, value_tile, jnp.zeros((1, 256), F32))
    kept = jnp.where(c == 0, side[1], side_in[1])
    pair_sum = jnp.sum(total, axis=1, keepdims=True)
    pv_own[...] = -kept * (jnp.broadcast_to(pair_sum, kept.shape) / (virtuals * virtuals))
    pv_copy = remote(pv_own, pv_in, pv_sem.at[0], pv_sem.at[1], back, n)
    pv_copy.start()

    scale = kept[:1, :1] * dens_scale

    core_copies = [None] * NX
    quarters = [((x // 2 + 1 + d // 2) % 2) * 2 + (x + d + d // 2) % 2 for d in range(NX)]
    for d in range(NX):
        q = quarters[d]
        if d % 2 == 0:
            half_cols = q // 2

            def dens_tile(ra, carry):
                rows = pl.ds(pl.multiple_of(ra * 256, 256), 256)
                cols = pl.ds(pl.multiple_of(half_cols * 256, 256), 256)
                dens = dot3(c_hi[rows, :], c_lo[rows, :], c_hi[cols, :], c_lo[cols, :]) * scale
                for k in range(4):
                    for e in range(2):
                        dbuf[half_cols * 2 + e, k % 2, ra * 2 + k // 2] = dens[k * 64:k * 64 + 64, e * 128:e * 128 + 128]
                return carry

            lax.fori_loop(0, 2, dens_tile, 0)
        copy = remote(dbuf.at[q, 1 - c], dpart.at[q], c_s.at[d], c_r.at[d], w, 2 * y + 1 - c)
        copy.start()
        core_copies[d] = copy
    x_copies = []
    for copy, d in zip(core_copies, range(NX)):
        q = quarters[d]
        copy.wait_recv()
        s0[q] = dbuf[q, c] + dpart[q]
        if d < NX - 1:
            out = remote(s0.at[q], xbuf.at[x], xs_s.at[d], xs_r.at[d], hi * PLANE + q * NZ + z, n)
            out.start()
            x_copies.append(out)
    for copy in x_copies:
        copy.wait_recv()
    xbuf[x] = s0[x]
    sum_x = ((xbuf[0] + xbuf[1]) + xbuf[2]) + xbuf[3]
    for k in range(NZ):
        s1[k] = sum_x[:, k * 8:k * 8 + 8, :]

    z_copies = []
    for d in range(1, NZ):
        copy = remote(s1.at[(z + d) % NZ], zbuf.at[d], zs_s.at[d], zs_r.at[d], at_z(d), n)
        copy.start()
        z_copies.append(copy)
    for copy in z_copies:
        copy.wait_recv()
    sum_z = s1[z]
    for d in range(1, NZ):
        sum_z = sum_z + zbuf[d]
    s2[...] = sum_z

    y_copies = []
    for d in range(1, 2 * NY):
        wide, narrow = at_y(d)
        copy = remote(s2.at[(y + d) % NY], ybuf.at[gy], ys_s.at[d], ys_r.at[d], wide, narrow)
        copy.start()
        y_copies.append(copy)
    ybuf[gy] = s2[y]
    for copy in y_copies:
        copy.wait_recv()
    sum_y = ybuf[0]
    for k in range(1, 2 * NY):
        sum_y = sum_y + ybuf[k]
    tbuf[...] = sum_y

    rows = pl.ds(pl.multiple_of(z * 8, 8), 8)
    cols = pl.ds(pl.multiple_of(x * 128, 128), 128)
    gz = []
    for d in range(1, PLANE):
        copy = remote(
            tbuf, ofull.at[rows, cols], gz_s.at[d], gz_r.at[d],
            hi * PLANE + ((x + d // NZ) % NX) * NZ + (z + d % NZ) % NZ, n,
        )
        copy.start()
        gz.append(copy)
    ofull[rows, cols] = sum_y
    pv_copy.wait()
    energy_out[...] = pv_own[...] + pv_in[...]
    for copy in gz:
        copy.wait_recv()
    dens_out[...] = ofull[...]

    for source, target, parity, columns in routes:
        for column, j, core in columns:
            @pl.when((plane == source) & takes(core))
            def _():
                remote(raw.at[0], relay_buf, b_s.at[j], b_r.at[0], hi * PLANE + column, n).wait_send()

            @pl.when((plane == column) & takes(core))
            def _():
                second_leg(target, parity, j).wait_send()

    @pl.when(sends_on)
    def _():
        for copy in forwards:
            copy.wait_send()

    for way in (0, 1):
        on_around_x(way).wait_send()
        for piece in (0, 1):
            around_x(way, piece).wait_send()

    for copy in m1 + [m_z] + m3 + a2a[1:] + core_copies + x_copies + z_copies + y_copies + gz:
        copy.wait_send()


def on_device(n_wide, raw_ints, metric, occ_energy, vir_energy, pair_kept):
    orbitals, vir_local, aux = raw_ints.shape
    virtuals = vir_energy.shape[0]
    dens_scale = 0.0625 / (n_wide * NARROW)
    side = jnp.stack([occ_energy, pair_kept.astype(F32)])[:, :, None]
    side = jnp.broadcast_to(side, (2, 8, 128))
    dma = pltpu.SemaphoreType.DMA
    vmem = pltpu.VMEM
    fit_shape = (orbitals, vir_local, aux)
    scratch = [
        vmem(fit_shape, F32), vmem(fit_shape, F32), vmem((aux, aux), F32),
        vmem((aux, aux), BF16), vmem((aux, aux), BF16),
        vmem((256, aux), BF16), vmem((256, aux), BF16),
        vmem(fit_shape, BF16), vmem(fit_shape, BF16), vmem(fit_shape, BF16), vmem(fit_shape, BF16),
        vmem((virtuals, virtuals), F32), vmem((virtuals, virtuals), F32), vmem((virtuals, virtuals), F32),
        vmem((virtuals, 2 * virtuals), BF16), vmem((virtuals, 2 * virtuals), BF16),
        vmem((NX, 2, NY, 64, 128), F32), vmem((NX, NY, 64, 128), F32), vmem((NX, NY, 64, 128), F32),
        vmem((NX, NY, 64, 128), F32),
        vmem((NZ, NY, 8, 128), F32), vmem((NZ, NY, 8, 128), F32), vmem((NY, 8, 128), F32),
        vmem((2 * NY, 8, 128), F32), vmem((8, 128), F32), vmem((vir_local, virtuals), F32),
        vmem((2, 8, 128), F32), vmem((8, 128), F32), vmem((8, 128), F32),
        vmem((vir_local, aux), F32), dma((4,)), dma((1,)), dma((1,)),
        dma((2,)), dma((8,)), dma((8,)), dma((8,)), dma((8,)),
        dma((4,)), dma((4,)), dma((6,)), dma((6,)), dma((4,)), dma((4,)), dma((2,)), dma((2,)),
        dma((4,)), dma((4,)), dma((4,)), dma((4,)), dma((8,)), dma((8,)), dma((8,)), dma((8,)),
        dma((32,)), dma((32,)),
    ]
    in_hbm = pl.BlockSpec(memory_space=pltpu.HBM)
    in_vmem = pl.BlockSpec(memory_space=pltpu.VMEM)
    density, energy = pl.pallas_call(
        functools.partial(kernel, n_wide, dens_scale),
        out_shape=(
            jax.ShapeDtypeStruct((vir_local, virtuals), F32),
            jax.ShapeDtypeStruct((8, 128), F32),
        ),
        in_specs=[in_hbm, in_hbm, in_vmem, in_vmem],
        out_specs=(in_vmem, in_vmem),
        scratch_shapes=scratch,
        compiler_params=pltpu.CompilerParams(
            collective_id=0, has_side_effects=True, vmem_limit_bytes=48 << 20
        ),
        name="pair_density",
    )(raw_ints, metric, side, vir_energy[None, :])
    return density, energy[0, :1]


def solution(mesh):
    placed = (
        P("wide", "narrow", None),
        P("narrow", None),
        P(("wide", "narrow")),
        P(),
        P(("wide", "narrow")),
    )
    return jax.shard_map(
        functools.partial(on_device, mesh.shape["wide"]),
        mesh=mesh,
        in_specs=placed,
        out_specs=(P("narrow", None), P(("wide", "narrow"))),
        check_vma=False,
    )
```

```python
import functools

import jax
import jax.numpy as jnp
from jax import lax
from jax.experimental import pallas as pl
from jax.experimental.pallas import tpu as pltpu
from jax.sharding import PartitionSpec as P

MESH = pl.DeviceIdType.MESH
F32 = jnp.float32
BF16 = jnp.bfloat16

NX, NZ, NY, NARROW = 4, 8, 4, 8
PLANE = NX * NZ
LAST, FIRST = PLANE - 1, 0
UP_COLUMNS = ((24, 3, None), (6, 1, 0), (30, 1, 1), (26, 0, 0), (2, 0, 1), (4, 2, 0), (28, 2, 1))
DOWN_COLUMNS = tuple((LAST - column, j, core) for column, j, core in UP_COLUMNS)


def split(value):
    high = value.astype(BF16)
    return high, (value - high.astype(F32)).astype(BF16)


def dot_nt(left, right):
    return lax.dot_general(left, right, (((1,), (1,)), ((), ())), preferred_element_type=F32)


def dot3(left_hi, left_lo, right_hi, right_lo):
    return dot_nt(left_hi, right_hi) + (dot_nt(left_hi, right_lo) + dot_nt(left_lo, right_hi))


def kernel(
    n_wide, dens_scale,
    raw, metric, side, vir,
    dens_out, energy_out,
    rbuf, jbuf, mbuf, m_hi, m_lo, x_hi, x_lo, fi_hi, fi_lo, fj_hi, fj_lo,
    rinv, pbuf, abuf, c_hi, c_lo, dbuf, dpart, s0, xbuf, s1, zbuf, s2, ybuf, tbuf, ofull,
    side_in, pv_own, pv_in,
    relay_buf, b_s, b_r, r_s,
    loc_sem, a_s, a_r, f_s, f_r, m1_s, m1_r, m2_s, m2_r, m3_s, m3_r, side_sem, pv_sem,
    c_s, c_r, xs_s, xs_r, zs_s, zs_r, ys_s, ys_r, gz_s, gz_r,
):
    w = lax.axis_index("wide")
    n = lax.axis_index("narrow")
    y, c = n // 2, n % 2
    hi, plane = w // PLANE, w % PLANE
    x, z = plane // NZ, plane % NZ
    gy = hi * NY + y
    up = (w + 1) % n_wide
    down = (w + n_wide - 1) % n_wide
    fwd = (w + 1 - 2 * c + n_wide) % n_wide
    back = (w - 1 + 2 * c + n_wide) % n_wide

    def remote(src, dst, ss, rs, wide, narrow):
        return pltpu.make_async_remote_copy(
            src_ref=src, dst_ref=dst, send_sem=ss, recv_sem=rs,
            device_id=(wide, narrow), device_id_type=MESH,
        )

    def at_x(d):
        return hi * PLANE + ((x + d) % NX) * NZ + z

    def at_z(d):
        return hi * PLANE + x * NZ + (z + d) % NZ

    def at_y(d):
        there = (gy + d) % (2 * NY)
        return (there // NY) * PLANE + plane, 2 * (there % NY) + c

    peers = [(w, (n + d) % NARROW) for d in range(1, NARROW)]
    peers += [at_y(d) for d in range(1, 2 * NY)]
    peers += [
        (hi * PLANE + ((x + d // NZ) % NX) * NZ + (z + d % NZ) % NZ, n) for d in range(1, PLANE)
    ]
    peers += [(up, n), (down, n)]
    barrier = pltpu.get_barrier_semaphore()

    def greet(wide, narrow):
        pl.semaphore_signal(barrier, inc=1, device_id=(wide, narrow), device_id_type=MESH)

    for peer in peers:
        greet(*peer)
    routes = ((LAST, FIRST, 0, UP_COLUMNS), (FIRST, LAST, 1, DOWN_COLUMNS))
    sends_on = jnp.logical_not(((plane == LAST) & (c == 0)) | ((plane == FIRST) & (c == 1)))
    def takes(core):
        return c == c if core is None else c == core

    for source, target, parity, columns in routes:
        for column, j, core in columns:
            @pl.when((plane == source) & takes(core))
            def _():
                greet(hi * PLANE + column, n)

            @pl.when((plane == column) & takes(core))
            def _():
                greet(hi * PLANE + source, n)
                greet((1 - hi) * PLANE + target, 2 * ((j + NY - y) % NY) + parity)

            @pl.when((plane == target) & (c == parity))
            def _():
                for from_core in (0, 1) if core is None else (core,):
                    greet((1 - hi) * PLANE + column, 2 * ((j + NY - y) % NY) + from_core)

    at_end = (plane == LAST) | (plane == FIRST)
    on_way = plane < 0
    for column, j, core in UP_COLUMNS + DOWN_COLUMNS:
        on_way = on_way | ((plane == column) & takes(core))
    for case, more in (
        (at_end & sends_on, NY + NARROW),
        (at_end & jnp.logical_not(sends_on), NY),
        (on_way, 2),
        (jnp.logical_not(at_end | on_way), 0),
    ):
        @pl.when(case)
        def _():
            pl.semaphore_wait(barrier, len(peers) + more)

    rows_q = metric.shape[0] // NX
    half_aux = metric.shape[1] // 2
    block = NY * rows_q
    half = NX * block
    mine = z % 2

    def aux_half(piece):
        return pl.ds(pl.multiple_of(piece * half_aux, half_aux), half_aux)

    share = metric.at[pl.ds(x * rows_q, rows_q), aux_half(mine)]
    own_part = mbuf.at[pl.ds(x * block + y * rows_q, rows_q), aux_half(mine)]
    m1 = []
    for d in range(1, NY):
        copy = remote(share, own_part, m1_s.at[d], m1_r.at[d], w, 2 * ((y + d) % NY) + c)
        copy.start()
        m1.append(copy)
    m_local = pltpu.make_async_copy(share, own_part, loc_sem.at[0])
    m_local.start()
    side_copy = remote(side, side_in, side_sem.at[0], side_sem.at[1], fwd, n)
    side_copy.start()

    for source, target, parity, columns in routes:
        for column, j, core in columns:
            @pl.when((plane == source) & takes(core))
            def _():
                k = (j + NY - y) % NY
                remote(
                    raw.at[2 * k + parity], relay_buf, b_s.at[j], b_r.at[0], hi * PLANE + column, n
                ).start()

    a2a = [None]
    for d in range(1, NARROW):
        to = (n + d) % NARROW
        copy = remote(raw.at[to], rbuf.at[n], a_s.at[d], a_r.at[d], w, to)
        copy.start()
        a2a.append(copy)
    own_slot = pltpu.make_async_copy(raw.at[n], rbuf.at[n], loc_sem.at[1])
    own_slot.start()
    slots = [(n + NARROW - d) % NARROW for d in range(NARROW)]
    forwards = []

    def forward(d):
        src = raw.at[n] if d == 0 else rbuf.at[slots[d]]
        copy = remote(src, jbuf.at[slots[d]], f_s.at[d], f_r.at[d], fwd, n)
        forwards.append(copy)

        @pl.when(sends_on)
        def _():
            copy.start()

    forward(0)
    a2a[1].wait_recv()
    forward(1)

    def second_leg(target, parity, j):
        to = 2 * ((j + NY - y) % NY) + parity
        return remote(
            relay_buf, jbuf.at[n], r_s.at[0], f_r.at[(to + NARROW - n) % NARROW], (1 - hi) * PLANE + target, to
        )

    for source, target, parity, columns in routes:
        for column, j, core in columns:
            @pl.when((plane == column) & takes(core))
            def _():
                remote(raw.at[0], relay_buf, b_s.at[j], b_r.at[0], hi * PLANE + source, n).wait_recv()
                second_leg(target, parity, j).start()

    m_local.wait()
    for copy in m1:
        copy.wait_recv()

    def m_piece(which, piece):
        return mbuf.at[pl.ds(which * block, block), aux_half(piece)]

    def around_x(way, piece):
        src = m_piece(x, piece)
        k = 2 * way + piece
        return remote(src, src, m2_s.at[k], m2_r.at[k], at_x(1 - 2 * way + NX), n)

    def on_around_x(way):
        src = m_piece((x + NX - 1 + 2 * way) % NX, way)
        return remote(src, src, m2_s.at[4 + way], m2_r.at[4 + way], at_x(1 - 2 * way + NX), n)

    m_z = remote(
        m_piece(x, mine), m_piece(x, mine), m1_s.at[0], m1_r.at[0], hi * PLANE + x * NZ + z + 1 - 2 * mine, n
    )
    m_z.start()
    for way in (0, 1):
        around_x(way, mine).start()
    m3 = []

    def to_partner(d):
        which = (x + d) % NX
        copy = remote(
            mbuf.at[pl.ds(which * block, block)], mbuf.at[pl.ds(half + which * block, block)],
            m3_s.at[d], m3_r.at[d], w, 2 * y + 1 - c,
        )
        copy.start()
        m3.append(copy)

    side_copy.wait()
    virtuals = vir.shape[1]
    pbuf[...] = jnp.broadcast_to(vir[...], (virtuals, virtuals))
    energies = side[0][:1, :1] + side_in[0][:1, :1]
    for r in range(0, virtuals, 128):
        across = pbuf[:, r:r + 128].T
        rinv[r:r + 128, :] = 1.0 / ((pbuf[r:r + 128, :] + across) - energies)

    for d in (2, 3):
        a2a[d].wait_recv()
        forward(d)
    m_z.wait_recv()
    for way in (0, 1):
        around_x(way, 1 - mine).start()
    to_partner(0)
    a2a[4].wait_recv()
    forward(4)
    for way in (0, 1):
        around_x(way, way).wait_recv()
        on_around_x(way).start()
    a2a[5].wait_recv()
    forward(5)
    for way in (0, 1):
        around_x(way, 1 - way).wait_recv()
        to_partner(3 - 2 * way)
    for way in (0, 1):
        on_around_x(way).wait_recv()
    to_partner(2)
    a2a[6].wait_recv()
    forward(6)
    for copy in m3:
        copy.wait_recv()

    def split_rows(k, carry):
        rows = pl.ds(pl.multiple_of(k * 96, 96), 96)
        m_hi[rows, :], m_lo[rows, :] = split(mbuf[rows, :])
        return carry

    lax.fori_loop(0, mbuf.shape[0] // 96, split_rows, 0)

    def fit(src, f_hi, f_lo, four):
        for k, slot in enumerate(four):
            part = pl.ds(k * 64, 64)
            x_hi[part, :], x_lo[part, :] = split(src[slot])

        def tile(t, carry):
            cols = pl.ds(pl.multiple_of(t * 256, 256), 256)
            fitted = dot3(x_hi[...], x_lo[...], m_hi[cols, :], m_lo[cols, :])
            high, low = split(fitted)
            for k, slot in enumerate(four):
                f_hi[slot, :, cols] = high[k * 64:(k + 1) * 64]
                f_lo[slot, :, cols] = low[k * 64:(k + 1) * 64]
            return carry

        lax.fori_loop(0, mbuf.shape[0] // 256, tile, 0)

    own_slot.wait()
    a2a[7].wait_recv()
    forward(7)
    fit(rbuf, fi_hi, fi_lo, slots[:4])
    for d in range(4):
        forwards[d].wait_recv()
    fit(jbuf, fj_hi, fj_lo, slots[:4])
    fit(rbuf, fi_hi, fi_lo, slots[4:])

    def pair_rows(four):
        for k, slot in enumerate(four):
            part = pl.ds(k * 64, 64)
            x_hi[part, :] = fj_hi[slot]
            x_lo[part, :] = fj_lo[slot]

        def tile(cb, carry):
            four_b = pl.ds(cb * 4, 4)
            shape = (256, fi_hi.shape[2])
            ints = dot3(x_hi[...], x_lo[...], fi_hi[four_b].reshape(shape), fi_lo[four_b].reshape(shape))
            cols = pl.ds(pl.multiple_of(cb * 256, 256), 256)
            for k, slot in enumerate(four):
                rows = pl.ds(pl.multiple_of(slot * 64, 64), 64)
                part = ints[k * 64:(k + 1) * 64]
                pbuf[rows, cols] = part
                abuf[rows, cols] = part * rinv[rows, cols]
            return carry

        lax.fori_loop(0, 2, tile, 0)

    pair_rows(slots[:4])
    for d in range(4, 8):
        forwards[d].wait_recv()
    fit(jbuf, fj_hi, fj_lo, slots[4:])
    pair_rows(slots[4:])

    def value_tile(t, total):
        ra, cb = t // 2, t % 2
        rows = pl.ds(pl.multiple_of(ra * 256, 256), 256)
        cols = pl.ds(pl.multiple_of(cb * 256, 256), 256)
        cols_t = pl.ds(pl.multiple_of(virtuals + cb * 256, 256), 256)
        amp = abuf[rows, cols]
        amp_t = abuf[cols, rows].T
        c_hi[rows, cols], c_lo[rows, cols] = split(amp)
        c_hi[rows, cols_t], c_lo[rows, cols_t] = split(amp_t)
        return total + jnp.sum(pbuf[rows, cols] * (2.0 * amp - amp_t), axis=0, keepdims=True)

    total = lax.fori_loop(0, 4, value_tile, jnp.zeros((1, 256), F32))
    kept = jnp.where(c == 0, side[1], side_in[1])
    pair_sum = jnp.sum(total, axis=1, keepdims=True)
    pv_own[...] = -kept * (jnp.broadcast_to(pair_sum, kept.shape) / (virtuals * virtuals))
    pv_copy = remote(pv_own, pv_in, pv_sem.at[0], pv_sem.at[1], back, n)
    pv_copy.start()

    scale = kept[:1, :1] * dens_scale

    core_copies = [None] * NX
    quarters = [((x // 2 + 1 + d // 2) % 2) * 2 + (x + d + d // 2) % 2 for d in range(NX)]
    for d in range(NX):
        q = quarters[d]
        if d % 2 == 0:
            half_cols = q // 2

            def dens_tile(ra, carry):
                rows = pl.ds(pl.multiple_of(ra * 256, 256), 256)
                cols = pl.ds(pl.multiple_of(half_cols * 256, 256), 256)
                dens = dot3(c_hi[rows, :], c_lo[rows, :], c_hi[cols, :], c_lo[cols, :]) * scale
                for k in range(4):
                    for e in range(2):
                        dbuf[half_cols * 2 + e, k % 2, ra * 2 + k // 2] = dens[k * 64:k * 64 + 64, e * 128:e * 128 + 128]
                return carry

            lax.fori_loop(0, 2, dens_tile, 0)
        copy = remote(dbuf.at[q, 1 - c], dpart.at[q], c_s.at[d], c_r.at[d], w, 2 * y + 1 - c)
        copy.start()
        core_copies[d] = copy
    x_copies = []
    for copy, d in zip(core_copies, range(NX)):
        q = quarters[d]
        copy.wait_recv()
        s0[q] = dbuf[q, c] + dpart[q]
        if d < NX - 1:
            out = remote(s0.at[q], xbuf.at[x], xs_s.at[d], xs_r.at[d], hi * PLANE + q * NZ + z, n)
            out.start()
            x_copies.append(out)
    for copy in x_copies:
        copy.wait_recv()
    xbuf[x] = s0[x]
    sum_x = ((xbuf[0] + xbuf[1]) + xbuf[2]) + xbuf[3]
    for k in range(NZ):
        s1[k] = sum_x[:, k * 8:k * 8 + 8, :]

    z_copies = []
    for d in range(1, NZ):
        copy = remote(s1.at[(z + d) % NZ], zbuf.at[d], zs_s.at[d], zs_r.at[d], at_z(d), n)
        copy.start()
        z_copies.append(copy)
    for copy in z_copies:
        copy.wait_recv()
    sum_z = s1[z]
    for d in range(1, NZ):
        sum_z = sum_z + zbuf[d]
    s2[...] = sum_z

    y_copies = []
    for d in range(1, 2 * NY):
        wide, narrow = at_y(d)
        copy = remote(s2.at[(y + d) % NY], ybuf.at[gy], ys_s.at[d], ys_r.at[d], wide, narrow)
        copy.start()
        y_copies.append(copy)
    ybuf[gy] = s2[y]
    for copy in y_copies:
        copy.wait_recv()
    sum_y = ybuf[0]
    for k in range(1, 2 * NY):
        sum_y = sum_y + ybuf[k]
    tbuf[...] = sum_y

    rows = pl.ds(pl.multiple_of(z * 8, 8), 8)
    cols = pl.ds(pl.multiple_of(x * 128, 128), 128)
    gz = []
    for d in range(1, PLANE):
        copy = remote(
            tbuf, ofull.at[rows, cols], gz_s.at[d], gz_r.at[d],
            hi * PLANE + ((x + d // NZ) % NX) * NZ + (z + d % NZ) % NZ, n,
        )
        copy.start()
        gz.append(copy)
    ofull[rows, cols] = sum_y
    pv_copy.wait()
    energy_out[...] = pv_own[...] + pv_in[...]
    for copy in gz:
        copy.wait_recv()
    dens_out[...] = ofull[...]

    for source, target, parity, columns in routes:
        for column, j, core in columns:
            @pl.when((plane == source) & takes(core))
            def _():
                remote(raw.at[0], relay_buf, b_s.at[j], b_r.at[0], hi * PLANE + column, n).wait_send()

            @pl.when((plane == column) & takes(core))
            def _():
                second_leg(target, parity, j).wait_send()

    @pl.when(sends_on)
    def _():
        for copy in forwards:
            copy.wait_send()

    for way in (0, 1):
        on_around_x(way).wait_send()
        for piece in (0, 1):
            around_x(way, piece).wait_send()

    for copy in m1 + [m_z] + m3 + a2a[1:] + core_copies + x_copies + z_copies + y_copies + gz:
        copy.wait_send()


def on_device(n_wide, raw_ints, metric, occ_energy, vir_energy, pair_kept):
    orbitals, vir_local, aux = raw_ints.shape
    virtuals = vir_energy.shape[0]
    dens_scale = 0.0625 / (n_wide * NARROW)
    side = jnp.stack([occ_energy, pair_kept.astype(F32)])[:, :, None]
    side = jnp.broadcast_to(side, (2, 8, 128))
    dma = pltpu.SemaphoreType.DMA
    vmem = pltpu.VMEM
    fit_shape = (orbitals, vir_local, aux)
    scratch = [
        vmem(fit_shape, F32), vmem(fit_shape, F32), vmem((aux, aux), F32),
        vmem((aux, aux), BF16), vmem((aux, aux), BF16),
        vmem((256, aux), BF16), vmem((256, aux), BF16),
        vmem(fit_shape, BF16), vmem(fit_shape, BF16), vmem(fit_shape, BF16), vmem(fit_shape, BF16),
        vmem((virtuals, virtuals), F32), vmem((virtuals, virtuals), F32), vmem((virtuals, virtuals), F32),
        vmem((virtuals, 2 * virtuals), BF16), vmem((virtuals, 2 * virtuals), BF16),
        vmem((NX, 2, NY, 64, 128), F32), vmem((NX, NY, 64, 128), F32), vmem((NX, NY, 64, 128), F32),
        vmem((NX, NY, 64, 128), F32),
        vmem((NZ, NY, 8, 128), F32), vmem((NZ, NY, 8, 128), F32), vmem((NY, 8, 128), F32),
        vmem((2 * NY, 8, 128), F32), vmem((8, 128), F32), vmem((vir_local, virtuals), F32),
        vmem((2, 8, 128), F32), vmem((8, 128), F32), vmem((8, 128), F32),
        vmem((vir_local, aux), F32), dma((4,)), dma((1,)), dma((1,)),
        dma((2,)), dma((8,)), dma((8,)), dma((8,)), dma((8,)),
        dma((4,)), dma((4,)), dma((6,)), dma((6,)), dma((4,)), dma((4,)), dma((2,)), dma((2,)),
        dma((4,)), dma((4,)), dma((4,)), dma((4,)), dma((8,)), dma((8,)), dma((8,)), dma((8,)),
        dma((32,)), dma((32,)),
    ]
    in_hbm = pl.BlockSpec(memory_space=pltpu.HBM)
    in_vmem = pl.BlockSpec(memory_space=pltpu.VMEM)
    density, energy = pl.pallas_call(
        functools.partial(kernel, n_wide, dens_scale),
        out_shape=(
            jax.ShapeDtypeStruct((vir_local, virtuals), F32),
            jax.ShapeDtypeStruct((8, 128), F32),
        ),
        in_specs=[in_hbm, in_hbm, in_vmem, in_vmem],
        out_specs=(in_vmem, in_vmem),
        scratch_shapes=scratch,
        compiler_params=pltpu.CompilerParams(
            collective_id=0, has_side_effects=True, vmem_limit_bytes=55500000
        ),
        name="pair_density",
    )(raw_ints, metric, side, vir_energy[None, :])
    return density, energy[0, :1]


def solution(mesh):
    placed = (
        P("wide", "narrow", None),
        P("narrow", None),
        P(("wide", "narrow")),
        P(),
        P(("wide", "narrow")),
    )
    return jax.shard_map(
        functools.partial(on_device, mesh.shape["wide"]),
        mesh=mesh,
        in_specs=placed,
        out_specs=(P("narrow", None), P(("wide", "narrow"))),
        check_vma=False,
    )
```

```python
import functools

import jax
import jax.numpy as jnp
from jax import lax
from jax.experimental import pallas as pl
from jax.experimental.pallas import tpu as pltpu
from jax.sharding import PartitionSpec as P

MESH = pl.DeviceIdType.MESH
F32 = jnp.float32
BF16 = jnp.bfloat16

NX, NZ, NY, NARROW = 4, 8, 4, 8
PLANE = NX * NZ
LAST, FIRST = PLANE - 1, 0
UP_COLUMNS = ((7, 3, None), (25, 1, 0), (1, 1, 1), (5, 0, 0), (29, 0, 1), (27, 2, 0), (3, 2, 1))
DOWN_COLUMNS = tuple((LAST - column, j, core) for column, j, core in UP_COLUMNS)


def split(value):
    high = value.astype(BF16)
    return high, (value - high.astype(F32)).astype(BF16)


def dot_nt(left, right):
    return lax.dot_general(left, right, (((1,), (1,)), ((), ())), preferred_element_type=F32)


def dot3(left_hi, left_lo, right_hi, right_lo):
    return dot_nt(left_hi, right_hi) + (dot_nt(left_hi, right_lo) + dot_nt(left_lo, right_hi))


def kernel(
    n_wide, dens_scale,
    raw, metric, side, vir,
    dens_out, energy_out,
    rbuf, jbuf, mbuf, m_hi, m_lo, x_hi, x_lo, fi_hi, fi_lo, fj_hi, fj_lo,
    rinv, pbuf, abuf, c_hi, c_lo, dbuf, dpart, s0, xbuf, s1, zbuf, s2, ybuf, tbuf, ofull,
    side_in, pv_own, pv_in,
    relay_buf, b_s, b_r, r_s,
    loc_sem, a_s, a_r, f_s, f_r, m1_s, m1_r, m2_s, m2_r, m3_s, m3_r, side_sem, pv_sem,
    c_s, c_r, xs_s, xs_r, zs_s, zs_r, ys_s, ys_r, gz_s, gz_r,
):
    w = lax.axis_index("wide")
    n = lax.axis_index("narrow")
    y, c = n // 2, n % 2
    hi, plane = w // PLANE, w % PLANE
    x, z = plane // NZ, plane % NZ
    gy = hi * NY + y
    up = (w + 1) % n_wide
    down = (w + n_wide - 1) % n_wide
    fwd = (w + 1 - 2 * c + n_wide) % n_wide
    back = (w - 1 + 2 * c + n_wide) % n_wide

    def remote(src, dst, ss, rs, wide, narrow):
        return pltpu.make_async_remote_copy(
            src_ref=src, dst_ref=dst, send_sem=ss, recv_sem=rs,
            device_id=(wide, narrow), device_id_type=MESH,
        )

    def at_x(d):
        return hi * PLANE + ((x + d) % NX) * NZ + z

    def at_z(d):
        return hi * PLANE + x * NZ + (z + d) % NZ

    def at_y(d):
        there = (gy + d) % (2 * NY)
        return (there // NY) * PLANE + plane, 2 * (there % NY) + c

    peers = [(w, (n + d) % NARROW) for d in range(1, NARROW)]
    peers += [at_y(d) for d in range(1, 2 * NY)]
    peers += [
        (hi * PLANE + ((x + d // NZ) % NX) * NZ + (z + d % NZ) % NZ, n) for d in range(1, PLANE)
    ]
    peers += [(up, n), (down, n)]
    barrier = pltpu.get_barrier_semaphore()

    def greet(wide, narrow):
        pl.semaphore_signal(barrier, inc=1, device_id=(wide, narrow), device_id_type=MESH)

    for peer in peers:
        greet(*peer)
    routes = ((LAST, FIRST, 0, UP_COLUMNS), (FIRST, LAST, 1, DOWN_COLUMNS))
    sends_on = jnp.logical_not(((plane == LAST) & (c == 0)) | ((plane == FIRST) & (c == 1)))
    def takes(core):
        return c == c if core is None else c == core

    for source, target, parity, columns in routes:
        for column, j, core in columns:
            @pl.when((plane == source) & takes(core))
            def _():
                greet(hi * PLANE + column, n)

            @pl.when((plane == column) & takes(core))
            def _():
                greet(hi * PLANE + source, n)
                greet((1 - hi) * PLANE + target, 2 * ((j + NY - y) % NY) + parity)

            @pl.when((plane == target) & (c == parity))
            def _():
                for from_core in (0, 1) if core is None else (core,):
                    greet((1 - hi) * PLANE + column, 2 * ((j + NY - y) % NY) + from_core)

    at_end = (plane == LAST) | (plane == FIRST)
    on_way = plane < 0
    for column, j, core in UP_COLUMNS + DOWN_COLUMNS:
        on_way = on_way | ((plane == column) & takes(core))
    for case, more in (
        (at_end & sends_on, NY + NARROW),
        (at_end & jnp.logical_not(sends_on), NY),
        (on_way, 2),
        (jnp.logical_not(at_end | on_way), 0),
    ):
        @pl.when(case)
        def _():
            pl.semaphore_wait(barrier, len(peers) + more)

    rows_q = metric.shape[0] // NX
    half_aux = metric.shape[1] // 2
    block = NY * rows_q
    half = NX * block
    mine = z % 2

    def aux_half(piece):
        return pl.ds(pl.multiple_of(piece * half_aux, half_aux), half_aux)

    share = metric.at[pl.ds(x * rows_q, rows_q), aux_half(mine)]
    own_part = mbuf.at[pl.ds(x * block + y * rows_q, rows_q), aux_half(mine)]
    m1 = []
    for d in range(1, NY):
        copy = remote(share, own_part, m1_s.at[d], m1_r.at[d], w, 2 * ((y + d) % NY) + c)
        copy.start()
        m1.append(copy)
    m_local = pltpu.make_async_copy(share, own_part, loc_sem.at[0])
    m_local.start()
    side_copy = remote(side, side_in, side_sem.at[0], side_sem.at[1], fwd, n)
    side_copy.start()

    for source, target, parity, columns in routes:
        for column, j, core in columns:
            @pl.when((plane == source) & takes(core))
            def _():
                k = (j + NY - y) % NY
                remote(
                    raw.at[2 * k + parity], relay_buf, b_s.at[j], b_r.at[0], hi * PLANE + column, n
                ).start()

    a2a = [None]
    parts = [pl.ds(0, raw.shape[1] // 2), pl.ds(raw.shape[1] // 2, raw.shape[1] // 2)]
    for d in range(1, NARROW):
        to = (n + d) % NARROW
        pair = [
            remote(raw.at[to, part], rbuf.at[n, part], a_s.at[2 * d + h], a_r.at[2 * d + h], w, to)
            for h, part in enumerate(parts)
        ]
        for copy in pair:
            copy.start()
        a2a.append(pair)
    own_slot = pltpu.make_async_copy(raw.at[n], rbuf.at[n], loc_sem.at[1])
    own_slot.start()
    slots = [(n + NARROW - d) % NARROW for d in range(NARROW)]
    forwards = []

    def forward(d):
        src = raw.at[n] if d == 0 else rbuf.at[slots[d]]
        pair = [
            remote(src.at[part], jbuf.at[slots[d], part], f_s.at[2 * d + h], f_r.at[2 * d + h], fwd, n)
            for h, part in enumerate(parts)
        ]
        forwards.append(pair)
        for h in range(2):
            if d:
                a2a[d][h].wait_recv()

            @pl.when(sends_on)
            def _():
                pair[h].start()

    forward(0)
    forward(1)

    def second_leg(target, parity, j):
        to = 2 * ((j + NY - y) % NY) + parity
        d = (to + NARROW - n) % NARROW
        return [
            remote(
                relay_buf.at[part], jbuf.at[n, part], r_s.at[h], f_r.at[2 * d + h], (1 - hi) * PLANE + target, to
            )
            for h, part in enumerate(parts)
        ]

    for source, target, parity, columns in routes:
        for column, j, core in columns:
            @pl.when((plane == column) & takes(core))
            def _():
                remote(raw.at[0], relay_buf, b_s.at[j], b_r.at[0], hi * PLANE + source, n).wait_recv()
                for copy in second_leg(target, parity, j):
                    copy.start()

    m_local.wait()
    for copy in m1:
        copy.wait_recv()

    def m_piece(which, piece):
        return mbuf.at[pl.ds(which * block, block), aux_half(piece)]

    def around_x(way, piece):
        src = m_piece(x, piece)
        k = 2 * way + piece
        return remote(src, src, m2_s.at[k], m2_r.at[k], at_x(1 - 2 * way + NX), n)

    def on_around_x(way):
        src = m_piece((x + NX - 1 + 2 * way) % NX, way)
        return remote(src, src, m2_s.at[4 + way], m2_r.at[4 + way], at_x(1 - 2 * way + NX), n)

    m_z = remote(
        m_piece(x, mine), m_piece(x, mine), m1_s.at[0], m1_r.at[0], hi * PLANE + x * NZ + z + 1 - 2 * mine, n
    )
    m_z.start()
    for way in (0, 1):
        around_x(way, mine).start()
    m3 = []

    def to_partner(d):
        which = (x + d) % NX
        copy = remote(
            mbuf.at[pl.ds(which * block, block)], mbuf.at[pl.ds(half + which * block, block)],
            m3_s.at[d], m3_r.at[d], w, 2 * y + 1 - c,
        )
        copy.start()
        m3.append(copy)

    side_copy.wait()
    virtuals = vir.shape[1]
    pbuf[...] = jnp.broadcast_to(vir[...], (virtuals, virtuals))
    energies = side[0][:1, :1] + side_in[0][:1, :1]
    for r in range(0, virtuals, 128):
        across = pbuf[:, r:r + 128].T
        rinv[r:r + 128, :] = 1.0 / ((pbuf[r:r + 128, :] + across) - energies)

    for d in (2, 3):
        forward(d)
    m_z.wait_recv()
    for way in (0, 1):
        around_x(way, 1 - mine).start()
    to_partner(0)
    forward(4)
    for way in (0, 1):
        around_x(way, way).wait_recv()
        on_around_x(way).start()
    forward(5)
    for way in (0, 1):
        around_x(way, 1 - way).wait_recv()
        to_partner(3 - 2 * way)
    for way in (0, 1):
        on_around_x(way).wait_recv()
    to_partner(2)
    forward(6)
    for copy in m3:
        copy.wait_recv()

    def split_rows(k, carry):
        rows = pl.ds(pl.multiple_of(k * 96, 96), 96)
        m_hi[rows, :], m_lo[rows, :] = split(mbuf[rows, :])
        return carry

    lax.fori_loop(0, mbuf.shape[0] // 96, split_rows, 0)

    def fit(src, f_hi, f_lo, four):
        for k, slot in enumerate(four):
            part = pl.ds(k * 64, 64)
            x_hi[part, :], x_lo[part, :] = split(src[slot])

        def tile(t, carry):
            cols = pl.ds(pl.multiple_of(t * 256, 256), 256)
            fitted = dot3(x_hi[...], x_lo[...], m_hi[cols, :], m_lo[cols, :])
            high, low = split(fitted)
            for k, slot in enumerate(four):
                f_hi[slot, :, cols] = high[k * 64:(k + 1) * 64]
                f_lo[slot, :, cols] = low[k * 64:(k + 1) * 64]
            return carry

        lax.fori_loop(0, mbuf.shape[0] // 256, tile, 0)

    own_slot.wait()
    forward(7)
    fit(rbuf, fi_hi, fi_lo, slots[:4])
    for d in range(4):
        for copy in forwards[d]:
            copy.wait_recv()
    fit(jbuf, fj_hi, fj_lo, slots[:4])
    fit(rbuf, fi_hi, fi_lo, slots[4:])

    def pair_rows(four):
        for k, slot in enumerate(four):
            part = pl.ds(k * 64, 64)
            x_hi[part, :] = fj_hi[slot]
            x_lo[part, :] = fj_lo[slot]

        def tile(cb, carry):
            four_b = pl.ds(cb * 4, 4)
            shape = (256, fi_hi.shape[2])
            ints = dot3(x_hi[...], x_lo[...], fi_hi[four_b].reshape(shape), fi_lo[four_b].reshape(shape))
            cols = pl.ds(pl.multiple_of(cb * 256, 256), 256)
            for k, slot in enumerate(four):
                rows = pl.ds(pl.multiple_of(slot * 64, 64), 64)
                part = ints[k * 64:(k + 1) * 64]
                pbuf[rows, cols] = part
                abuf[rows, cols] = part * rinv[rows, cols]
            return carry

        lax.fori_loop(0, 2, tile, 0)

    pair_rows(slots[:4])
    for d in range(4, 8):
        for copy in forwards[d]:
            copy.wait_recv()
    fit(jbuf, fj_hi, fj_lo, slots[4:])
    pair_rows(slots[4:])

    def value_tile(t, total):
        ra, cb = t // 2, t % 2
        rows = pl.ds(pl.multiple_of(ra * 256, 256), 256)
        cols = pl.ds(pl.multiple_of(cb * 256, 256), 256)
        cols_t = pl.ds(pl.multiple_of(virtuals + cb * 256, 256), 256)
        amp = abuf[rows, cols]
        amp_t = abuf[cols, rows].T
        c_hi[rows, cols], c_lo[rows, cols] = split(amp)
        c_hi[rows, cols_t], c_lo[rows, cols_t] = split(amp_t)
        return total + jnp.sum(pbuf[rows, cols] * (2.0 * amp - amp_t), axis=0, keepdims=True)

    total = lax.fori_loop(0, 4, value_tile, jnp.zeros((1, 256), F32))
    kept = jnp.where(c == 0, side[1], side_in[1])
    pair_sum = jnp.sum(total, axis=1, keepdims=True)
    pv_own[...] = -kept * (jnp.broadcast_to(pair_sum, kept.shape) / (virtuals * virtuals))
    pv_copy = remote(pv_own, pv_in, pv_sem.at[0], pv_sem.at[1], back, n)
    pv_copy.start()

    scale = kept[:1, :1] * dens_scale

    core_copies = [None] * NX
    quarters = [((x // 2 + 1 + d // 2) % 2) * 2 + (x + d + d // 2) % 2 for d in range(NX)]
    for d in range(NX):
        q = quarters[d]
        if d % 2 == 0:
            half_cols = q // 2

            def dens_tile(ra, carry):
                rows = pl.ds(pl.multiple_of(ra * 256, 256), 256)
                cols = pl.ds(pl.multiple_of(half_cols * 256, 256), 256)
                dens = dot3(c_hi[rows, :], c_lo[rows, :], c_hi[cols, :], c_lo[cols, :]) * scale
                for k in range(4):
                    for e in range(2):
                        dbuf[half_cols * 2 + e, k % 2, ra * 2 + k // 2] = dens[k * 64:k * 64 + 64, e * 128:e * 128 + 128]
                return carry

            lax.fori_loop(0, 2, dens_tile, 0)
        copy = remote(dbuf.at[q, 1 - c], dpart.at[q], c_s.at[d], c_r.at[d], w, 2 * y + 1 - c)
        copy.start()
        core_copies[d] = copy
    x_copies = []
    for copy, d in zip(core_copies, range(NX)):
        q = quarters[d]
        copy.wait_recv()
        s0[q] = dbuf[q, c] + dpart[q]
        if d < NX - 1:
            out = remote(s0.at[q], xbuf.at[x], xs_s.at[d], xs_r.at[d], hi * PLANE + q * NZ + z, n)
            out.start()
            x_copies.append(out)
    for copy in x_copies:
        copy.wait_recv()
    xbuf[x] = s0[x]
    sum_x = ((xbuf[0] + xbuf[1]) + xbuf[2]) + xbuf[3]
    for k in range(NZ):
        s1[k] = sum_x[:, k * 8:k * 8 + 8, :]

    z_copies = []
    for d in range(1, NZ):
        copy = remote(s1.at[(z + d) % NZ], zbuf.at[d], zs_s.at[d], zs_r.at[d], at_z(d), n)
        copy.start()
        z_copies.append(copy)
    for copy in z_copies:
        copy.wait_recv()
    sum_z = s1[z]
    for d in range(1, NZ):
        sum_z = sum_z + zbuf[d]
    s2[...] = sum_z

    y_copies = []
    for d in range(1, 2 * NY):
        wide, narrow = at_y(d)
        copy = remote(s2.at[(y + d) % NY], ybuf.at[gy], ys_s.at[d], ys_r.at[d], wide, narrow)
        copy.start()
        y_copies.append(copy)
    ybuf[gy] = s2[y]
    for copy in y_copies:
        copy.wait_recv()
    sum_y = ybuf[0]
    for k in range(1, 2 * NY):
        sum_y = sum_y + ybuf[k]
    tbuf[...] = sum_y

    rows = pl.ds(pl.multiple_of(z * 8, 8), 8)
    cols = pl.ds(pl.multiple_of(x * 128, 128), 128)
    gz = []
    for d in range(1, PLANE):
        copy = remote(
            tbuf, ofull.at[rows, cols], gz_s.at[d], gz_r.at[d],
            hi * PLANE + ((x + d // NZ) % NX) * NZ + (z + d % NZ) % NZ, n,
        )
        copy.start()
        gz.append(copy)
    ofull[rows, cols] = sum_y
    pv_copy.wait()
    energy_out[...] = pv_own[...] + pv_in[...]
    for copy in gz:
        copy.wait_recv()
    dens_out[...] = ofull[...]

    for source, target, parity, columns in routes:
        for column, j, core in columns:
            @pl.when((plane == source) & takes(core))
            def _():
                remote(raw.at[0], relay_buf, b_s.at[j], b_r.at[0], hi * PLANE + column, n).wait_send()

            @pl.when((plane == column) & takes(core))
            def _():
                for copy in second_leg(target, parity, j):
                    copy.wait_send()

    @pl.when(sends_on)
    def _():
        for pair in forwards:
            for copy in pair:
                copy.wait_send()

    for way in (0, 1):
        on_around_x(way).wait_send()
        for piece in (0, 1):
            around_x(way, piece).wait_send()

    for copy in m1 + [m_z] + m3 + sum(a2a[1:], []) + core_copies + x_copies + z_copies + y_copies + gz:
        copy.wait_send()


def on_device(n_wide, raw_ints, metric, occ_energy, vir_energy, pair_kept):
    orbitals, vir_local, aux = raw_ints.shape
    virtuals = vir_energy.shape[0]
    dens_scale = 0.0625 / (n_wide * NARROW)
    side = jnp.stack([occ_energy, pair_kept.astype(F32)])[:, :, None]
    side = jnp.broadcast_to(side, (2, 8, 128))
    dma = pltpu.SemaphoreType.DMA
    vmem = pltpu.VMEM
    fit_shape = (orbitals, vir_local, aux)
    scratch = [
        vmem(fit_shape, F32), vmem(fit_shape, F32), vmem((aux, aux), F32),
        vmem((aux, aux), BF16), vmem((aux, aux), BF16),
        vmem((256, aux), BF16), vmem((256, aux), BF16),
        vmem(fit_shape, BF16), vmem(fit_shape, BF16), vmem(fit_shape, BF16), vmem(fit_shape, BF16),
        vmem((virtuals, virtuals), F32), vmem((virtuals, virtuals), F32), vmem((virtuals, virtuals), F32),
        vmem((virtuals, 2 * virtuals), BF16), vmem((virtuals, 2 * virtuals), BF16),
        vmem((NX, 2, NY, 64, 128), F32), vmem((NX, NY, 64, 128), F32), vmem((NX, NY, 64, 128), F32),
        vmem((NX, NY, 64, 128), F32),
        vmem((NZ, NY, 8, 128), F32), vmem((NZ, NY, 8, 128), F32), vmem((NY, 8, 128), F32),
        vmem((2 * NY, 8, 128), F32), vmem((8, 128), F32), vmem((vir_local, virtuals), F32),
        vmem((2, 8, 128), F32), vmem((8, 128), F32), vmem((8, 128), F32),
        vmem((vir_local, aux), F32), dma((4,)), dma((1,)), dma((2,)),
        dma((2,)), dma((16,)), dma((16,)), dma((16,)), dma((16,)),
        dma((4,)), dma((4,)), dma((6,)), dma((6,)), dma((4,)), dma((4,)), dma((2,)), dma((2,)),
        dma((4,)), dma((4,)), dma((4,)), dma((4,)), dma((8,)), dma((8,)), dma((8,)), dma((8,)),
        dma((32,)), dma((32,)),
    ]
    in_hbm = pl.BlockSpec(memory_space=pltpu.HBM)
    in_vmem = pl.BlockSpec(memory_space=pltpu.VMEM)
    density, energy = pl.pallas_call(
        functools.partial(kernel, n_wide, dens_scale),
        out_shape=(
            jax.ShapeDtypeStruct((vir_local, virtuals), F32),
            jax.ShapeDtypeStruct((8, 128), F32),
        ),
        in_specs=[in_hbm, in_hbm, in_vmem, in_vmem],
        out_specs=(in_vmem, in_vmem),
        scratch_shapes=scratch,
        compiler_params=pltpu.CompilerParams(
            collective_id=0, has_side_effects=True, vmem_limit_bytes=55500000
        ),
        name="pair_density",
    )(raw_ints, metric, side, vir_energy[None, :])
    return density, energy[0, :1]


def solution(mesh):
    placed = (
        P("wide", "narrow", None),
        P("narrow", None),
        P(("wide", "narrow")),
        P(),
        P(("wide", "narrow")),
    )
    return jax.shard_map(
        functools.partial(on_device, mesh.shape["wide"]),
        mesh=mesh,
        in_specs=placed,
        out_specs=(P("narrow", None), P(("wide", "narrow"))),
        check_vma=False,
    )
```
